256 devices in a mesh: space: 32 (over y_hi, z, core), coil: 8 (over y_lo, x).
Axes of the slice: x: 4, y: 4 (y_hi: 2, y_lo: 2; y = y_hi * 2 + y_lo), z: 8, core: 2. Of those that a mesh axis runs over, the one named last changes fastest.
Arguments:
- spatial_coef: bfloat16 [16, 128, 128, 2, 128], P('coil', 'space'), may hold values from -6 to 6
- temporal_basis: bfloat16 [2, 16, 4], replicated, may hold values from -1.5 to 1.5
- coil_maps: bfloat16 [32, 128, 128, 2, 128], P('coil', 'space'), may hold values from -6 to 6
- field_steps: int32 [128, 128, 128], P('space'), may hold values from 0 to 255
- kspace_data: bfloat16 [32, 4, 128, 128, 2, 128], P('coil', None, None, 'space'), may hold values from -6 to 6
- sample_mask: int32 [4, 128, 128], P(None, 'space'), may hold values 0 or 1
Outputs:
- gradient: float32 [16, 128, 128, 2, 128], P('coil', 'space')
The draws below stay inside these ranges and needn't reach their ends.
Inputs may be any that keep to these rules, and one draw needn't show every extreme that they name: `sample_mask`: 1 where a phase-encoding line is sampled at that point, else 0.
All inputs are finite; a program needn't handle non-finite values. No bound on the sum of `sample_mask` on one device may be relied on, other than what follows from the above.
Results may differ from the reference program's by a relative error of at most 0.014.
Values may be sent and summed in bfloat16 or wider, within the bound.
A program may use at most 64 MiB of HBM per device.

```python
import math
import jax
import jax.numpy as jnp
from jax import lax

NX = 128
NY = 128
NZ = 128
RANK = 16
PTS = 4
STEPS_CYCLE = 256
COILS = 32


def set_ends(drawn, stream_key, smallest, top_value):
    longest = drawn.shape.index(max(drawn.shape))
    spots = []
    for shift in (0, 1):
        where = [jax.random.randint(jax.random.fold_in(stream_key, axis), (), 0, length) for axis, length in enumerate(drawn.shape)]
        where[longest] = (where[longest] + shift) % drawn.shape[longest]
        spots.append(tuple(where))
    return drawn.at[spots[0]].set(smallest).at[spots[1]].set(top_value)


def block_levels(stream_key, dims, split, smallest, high):
    gain, own = 1.0, jax.random.fold_in(stream_key, 6)
    for position, blocks in split:
        steps = jnp.exp(jax.random.uniform(jax.random.fold_in(own, position), (blocks,), jnp.float32, smallest / len(split), high / len(split)))
        gain = gain * jnp.repeat(steps, dims[position] // blocks).reshape([-1 if axis == position else 1 for axis in range(len(dims))])
    return gain


def bell_draw(key, dims, deviation, limit, pieces=(), kind=jnp.bfloat16):
    factor_of = block_levels(key, dims, pieces, -0.22, 0.18) if pieces else 1.0
    result = jax.random.normal(key, dims, jnp.float32) * deviation * factor_of
    return jnp.minimum(jnp.maximum(result, -limit), limit).astype(kind)


def setup_inputs(seed: int = 0) -> dict:
    key_of = jax.random.split(jax.random.key(seed), 7)
    spatial_coef = bell_draw(key_of[0], (RANK, NX, NY, 2, NZ), 1.0, 6.0, ((0, 8), (1, 32)))
    temporal_basis = bell_draw(key_of[1], (2, RANK, PTS), RANK ** -0.5, 1.5)
    coil_maps = bell_draw(key_of[2], (COILS, NX, NY, 2, NZ), 0.5, 6.0, ((0, 8), (1, 32)))
    field_steps = set_ends(jax.random.randint(key_of[3], (NX, NY, NZ), 0, STEPS_CYCLE), jax.random.fold_in(key_of[3], 1), 0, STEPS_CYCLE - 1).astype(jnp.int32)
    kspace_data = bell_draw(key_of[4], (COILS, PTS, NX, NY, 2, NZ), 0.5, 6.0, ((0, 8), (3, 32)))
    sample_mask = set_ends((jax.random.randint(key_of[5], (PTS, NY, NZ), 0, 2) < 1).astype(jnp.int32), jax.random.fold_in(key_of[5], 1), 0, 1)
    return {"spatial_coef": spatial_coef, "temporal_basis": temporal_basis, "coil_maps": coil_maps, "field_steps": field_steps, "kspace_data": kspace_data, "sample_mask": sample_mask}


def dft_table(length, sign):
    index = jnp.arange(length, dtype=jnp.int32)
    steps = index[:, None] * index[None, :] % length
    angle = steps.astype(jnp.float32) * (2.0 * math.pi / length)
    scale = 1.0 / math.sqrt(length)
    cosine = jnp.cos(angle) * scale
    sine = jnp.sin(angle) * (sign * scale)
    upper = jnp.stack([cosine, sine], axis=1)
    lower = jnp.stack([-sine, cosine], axis=1)
    return jnp.stack([upper, lower], axis=0).astype(jnp.bfloat16)

def forward_mix(basis):
    real_part = basis[0]
    imaginary = basis[1]
    return jnp.stack([jnp.stack([real_part, imaginary], -1), jnp.stack([-imaginary, real_part], -1)], 1)

def adjoint_mix(basis):
    real_part = basis[0].T
    imaginary = basis[1].T
    return jnp.stack([jnp.stack([real_part, -imaginary], -1), jnp.stack([imaginary, real_part], -1)], 1)

def phase_parts(field_steps, points):
    counter = jnp.arange(1, points + 1, dtype=jnp.int32)
    steps = field_steps[None] * counter[:, None, None, None] % STEPS_CYCLE
    angle = steps.astype(jnp.float32) * (2.0 * math.pi / STEPS_CYCLE)
    return (jnp.cos(angle), jnp.sin(angle))

def transform(volume, table, form):
    return jnp.einsum(form, volume.astype(jnp.float32), table.astype(jnp.float32), precision=lax.Precision.HIGHEST)

def reference(spatial_coef, temporal_basis, coil_maps, field_steps, kspace_data, sample_mask):
    points = temporal_basis.shape[2]
    basis = temporal_basis.astype(jnp.float32)
    image = jnp.einsum('lxypz,lptq->txyqz', spatial_coef.astype(jnp.float32), forward_mix(basis), precision=lax.Precision.HIGHEST)
    cosine, sine = phase_parts(field_steps, points)
    image_real = image[:, :, :, 0]
    image_imaginary = image[:, :, :, 1]
    turned_real = cosine * image_real - sine * image_imaginary
    turned_imaginary = sine * image_real + cosine * image_imaginary
    depth_fwd = dft_table(NZ, -1.0)
    rows_fwd = dft_table(NY, -1.0)
    first_fwd = dft_table(NX, -1.0)
    depth_inv = dft_table(NZ, 1.0)
    rows_inv = dft_table(NY, 1.0)
    first_inv = dft_table(NX, 1.0)
    mask_float = sample_mask.astype(jnp.float32)[:, None, :, None, :]

    def per_coil(carry, items):
        maps, data = items
        map_real = maps[:, :, 0].astype(jnp.float32)
        map_imaginary = maps[:, :, 1].astype(jnp.float32)
        coil_real = map_real * turned_real - map_imaginary * turned_imaginary
        coil_imaginary = map_real * turned_imaginary + map_imaginary * turned_real
        coil_image = jnp.stack([coil_real, coil_imaginary], axis=3).astype(jnp.bfloat16)
        depth_pass = transform(coil_image, depth_fwd, 'txypz,pzqk->txyqk').astype(jnp.bfloat16)
        row_pass = transform(depth_pass, rows_fwd, 'txypz,pyqk->txkqz').astype(jnp.bfloat16)
        kspace = transform(row_pass, first_fwd, 'txypz,pxqk->tkyqz')
        residual = (mask_float * (kspace - data.astype(jnp.float32))).astype(jnp.bfloat16)
        back_first = transform(residual, first_inv, 'txypz,pxqk->tkyqz').astype(jnp.bfloat16)
        back_rows = transform(back_first, rows_inv, 'txypz,pyqk->txkqz').astype(jnp.bfloat16)
        back_image = transform(back_rows, depth_inv, 'txypz,pzqk->txyqk')
        back_real = back_image[:, :, :, 0]
        back_imaginary = back_image[:, :, :, 1]
        sum_real = carry[0] + (map_real * back_real + map_imaginary * back_imaginary)
        sum_imaginary = carry[1] + (map_real * back_imaginary - map_imaginary * back_real)
        return ((sum_real, sum_imaginary), None)
    zeros = jnp.zeros(turned_real.shape, jnp.float32)
    (sum_real, sum_imaginary), unused = lax.scan(per_coil, (zeros, zeros), (coil_maps, kspace_data))
    combined_real = cosine * sum_real + sine * sum_imaginary
    combined_imaginary = cosine * sum_imaginary - sine * sum_real
    combined = jnp.stack([combined_real, combined_imaginary], axis=3)
    return jnp.einsum('txypz,tplq->lxyqz', combined, adjoint_mix(basis), precision=lax.Precision.HIGHEST)
```

```python
import math

import jax
import jax.numpy as jnp
from jax import lax
from jax.sharding import PartitionSpec as P

STEPS_CYCLE = 256


def dft_table(length, sign):
    index = jnp.arange(length, dtype=jnp.int32)
    steps = index[:, None] * index[None, :] % length
    angle = steps.astype(jnp.float32) * (2.0 * math.pi / length)
    scale = 1.0 / math.sqrt(length)
    cosine = jnp.cos(angle) * scale
    sine = jnp.sin(angle) * (sign * scale)
    upper = jnp.stack([cosine, sine], axis=1)
    lower = jnp.stack([-sine, cosine], axis=1)
    return jnp.stack([upper, lower], axis=0).astype(jnp.bfloat16)


def forward_mix(basis):
    real_part = basis[0]
    imaginary = basis[1]
    return jnp.stack(
        [jnp.stack([real_part, imaginary], -1), jnp.stack([-imaginary, real_part], -1)], 1
    )


def adjoint_mix(basis):
    real_part = basis[0].T
    imaginary = basis[1].T
    return jnp.stack(
        [jnp.stack([real_part, -imaginary], -1), jnp.stack([imaginary, real_part], -1)], 1
    )


def phase_parts(field_steps, points):
    counter = jnp.arange(1, points + 1, dtype=jnp.int32)
    steps = field_steps[None] * counter[:, None, None, None] % STEPS_CYCLE
    angle = steps.astype(jnp.float32) * (2.0 * math.pi / STEPS_CYCLE)
    return (jnp.cos(angle), jnp.sin(angle))


def transform(volume, table, form):
    return jnp.einsum(form, volume, table, preferred_element_type=jnp.float32)


def shards(spatial_coef, temporal_basis, coil_maps, field_steps, kspace_data, sample_mask):
    points = temporal_basis.shape[2]
    section = temporal_basis
    data_first = transform(
        kspace_data, dft_table(kspace_data.shape[2], 1.0), "ctxypz,pxqk->ctkyqz"
    ).astype(jnp.bfloat16)
    measured = lax.all_to_all(data_first, "space", split_axis=2, concat_axis=3, tiled=True)
    mask_all = lax.all_gather(sample_mask.astype(jnp.bfloat16), "space", axis=1, tiled=True)
    mask_all = mask_all.astype(jnp.float32)[None, :, None, :, None, :]
    image = jnp.einsum(
        "lxypz,lptq->txyqz",
        lax.all_gather(spatial_coef, "coil", axis=0, tiled=True),
        forward_mix(section),
        preferred_element_type=jnp.float32,
    )
    cosine, sine = phase_parts(field_steps, points)
    image_real = image[:, :, :, 0]
    image_imaginary = image[:, :, :, 1]
    turned_real = cosine * image_real - sine * image_imaginary
    turned_imaginary = sine * image_real + cosine * image_imaginary
    map_real = coil_maps[:, :, :, 0].astype(jnp.float32)[:, None]
    map_imaginary = coil_maps[:, :, :, 1].astype(jnp.float32)[:, None]
    coil_real = map_real * turned_real - map_imaginary * turned_imaginary
    coil_imaginary = map_real * turned_imaginary + map_imaginary * turned_real
    coil_image = jnp.stack([coil_real, coil_imaginary], axis=4).astype(jnp.bfloat16)
    depth_count = coil_image.shape[5]
    row_count = coil_image.shape[3]
    depth_pass = transform(coil_image, dft_table(depth_count, -1.0), "ctxypz,pzqk->ctxyqk").astype(
        jnp.bfloat16
    )
    row_pass = transform(depth_pass, dft_table(row_count, -1.0), "ctxypz,pyqk->ctxkqz")
    residual = (mask_all * (row_pass - measured.astype(jnp.float32))).astype(jnp.bfloat16)
    back_rows = transform(residual, dft_table(row_count, 1.0), "ctxypz,pyqk->ctxkqz").astype(
        jnp.bfloat16
    )
    back_image = transform(back_rows, dft_table(depth_count, 1.0), "ctxypz,pzqk->ctxyqk")
    back_real = back_image[:, :, :, :, 0]
    back_imaginary = back_image[:, :, :, :, 1]
    sum_real = jnp.sum(map_real * back_real + map_imaginary * back_imaginary, axis=0)
    sum_imaginary = jnp.sum(map_real * back_imaginary - map_imaginary * back_real, axis=0)
    combined_real = cosine * sum_real + sine * sum_imaginary
    combined_imaginary = cosine * sum_imaginary - sine * sum_real
    combined = jnp.stack([combined_real, combined_imaginary], axis=3)
    section = temporal_basis.astype(jnp.float32)
    return lax.psum_scatter(
        jnp.einsum(
            "txypz,tplq->lxyqz", combined, adjoint_mix(section), precision=lax.Precision.HIGHEST
        ).astype(jnp.bfloat16),
        "coil",
        scatter_dimension=0,
        tiled=True,
    ).astype(jnp.float32)


def solution(mesh):
    in_specs = (
        P("coil", "space", None, None, None),
        P(),
        P("coil", "space", None, None, None),
        P("space", None, None),
        P("coil", None, None, "space", None, None),
        P(None, "space", None),
    )
    out_specs = P("coil", "space", None, None, None)
    return jax.shard_map(shards, mesh=mesh, in_specs=in_specs, out_specs=out_specs, check_vma=False)
```

```python
import functools
import math

import jax
import jax.numpy as jnp
import numpy as np
from jax import lax
from jax.experimental import pallas as pl
from jax.experimental.pallas import tpu as pltpu
from jax.sharding import PartitionSpec as P

STEPS_CYCLE = 256
N = 128
PTS = 4
LOCAL = 4
SLABS = 32
GROUPS = 8
ROWS = N // GROUPS
F32 = jnp.float32
BF16 = jnp.bfloat16
I32 = jnp.int32
MESH = pl.DeviceIdType.MESH


def dft_pair():
    index = np.arange(N)
    angle = (index[:, None] * index[None, :] % N).astype(np.float32) * np.float32(2.0 * math.pi / N)
    cosine = np.cos(angle) / np.float32(math.sqrt(N))
    sine = np.sin(angle) / np.float32(math.sqrt(N))
    inverse = np.block([[cosine, -sine], [sine, cosine]])
    return np.stack([inverse, inverse.T]).astype(jnp.bfloat16)


def dot(a, b):
    return jnp.dot(a, b, preferred_element_type=F32)


def iotas(rows, cols):
    return (
        lax.broadcasted_iota(I32, (rows, cols), 0),
        lax.broadcasted_iota(I32, (rows, cols), 1),
    )


def as_bf16(condition):
    return jnp.where(condition, 1.0, 0.0).astype(BF16)


def lanes(parts):
    return jnp.concatenate(parts, axis=1)


def rows_of(parts):
    return jnp.concatenate(parts, axis=0)


def body(
    coef_hbm, basis, maps_hbm, field_hbm, data_hbm, mask_hbm, table_hbm, out_ref,
    coef, maps, field, mask, table, data, mix_x, mix_y, send, recv, own_mask, all_mask, mask_full,
    sens_re, sens_im, cosine, sine, image_part, image_recv, image_all, model,
    comb_part, comb_recv, comb_all, grad,
    load_sem, data_sem, self_sem, send_sem, recv_sem, mask_send, mask_recv,
    irs_send, irs_recv, iag_send, iag_recv, crs_send, crs_recv, cag_send, cag_recv,
):
    me = lax.axis_index("space")
    mg = lax.axis_index("coil")

    barrier = pltpu.get_barrier_semaphore()

    def greet_space(k, carry):
        pl.semaphore_signal(barrier, inc=1, device_id=(lax.rem(me + k, SLABS), mg), device_id_type=MESH)
        return carry

    def greet_coil(k, carry):
        pl.semaphore_signal(barrier, inc=1, device_id=(me, lax.rem(mg + k, GROUPS)), device_id_type=MESH)
        return carry

    lax.fori_loop(1, SLABS, greet_space, 0)
    lax.fori_loop(1, GROUPS, greet_coil, 0)

    loads = [
        pltpu.make_async_copy(src, dst, load_sem.at[i])
        for i, (src, dst) in enumerate(
            [(table_hbm, table), (mask_hbm, mask), (coef_hbm, coef), (maps_hbm, maps), (field_hbm, field)]
        )
    ]

    def data_load(t, c):
        return pltpu.make_async_copy(
            data_hbm.at[c, t], data.at[t, :, pl.ds(c * N, N)], data_sem.at[t, c]
        )

    loads[0].start()
    loads[1].start()
    for c in range(LOCAL):
        data_load(0, c).start()
    for load in loads[2:]:
        load.start()
    for t in range(1, PTS):
        for c in range(LOCAL):
            data_load(t, c).start()
    loads[0].wait()

    row, col = iotas(2 * N, 8 * N)
    spread = as_bf16((row % N == col // 8) & (row // N == col % 2))
    wide = dot(table[0], spread).astype(BF16)
    row, col = iotas(2 * N, N // 2)
    repeat = as_bf16(col == row // 4)
    row, col = iotas(2 * N, 8 * N)
    same_line = row % 4 == (col // 2) % 4
    for block in range(4):
        part = dot(repeat, wide[block * (N // 2) : (block + 1) * (N // 2)])
        mix_x[pl.ds(block * 2 * N, 2 * N), :] = jnp.where(same_line, part, 0.0).astype(BF16)
    loads[1].wait()
    for t in range(PTS):
        own_mask[pl.ds(t * 4, 4), :] = mask[t].astype(F32).astype(BF16)

    def data_chunk(t):
        for c in range(LOCAL):
            data_load(t, c).wait()
        lines = mask[t].astype(F32)
        lines = rows_of([lines, lines])
        lines = lanes([lines] * LOCAL)
        for half in range(2):
            parts = []
            for p in range(2):
                mixed = dot(mix_x[pl.ds((2 * p + half) * 2 * N, 2 * N), :], data[t])
                mixed = mixed.reshape(32, 8, LOCAL * N) * lines[None]
                parts.append(mixed.reshape(2 * N, LOCAL * N).astype(BF16))
            stacked = rows_of(
                [lanes([parts[0][:, c * N : (c + 1) * N], parts[1][:, c * N : (c + 1) * N]]) for c in range(LOCAL)]
            )
            turned = dot(stacked, table[1]).astype(BF16)
            for c in range(LOCAL):
                piece = turned[c * 2 * N : (c + 1) * 2 * N]
                for p in range(2):
                    send[t, pl.ds(half * 16, 16), :, pl.ds((p * LOCAL + c) * N, N)] = piece[
                        :, p * N : (p + 1) * N
                    ].reshape(16, 16, N)

    def self_copy(t):
        return pltpu.make_async_copy(send.at[t, me], recv.at[t, me], self_sem.at[t])

    def push_data(t):
        self_copy(t).start()

        def push(k, carry):
            to = lax.rem(me + k, SLABS)
            pltpu.make_async_remote_copy(
                src_ref=send.at[t, to], dst_ref=recv.at[t, me],
                send_sem=send_sem.at[t], recv_sem=recv_sem.at[t],
                device_id=(to, mg), device_id_type=MESH,
            ).start()
            return carry

        lax.fori_loop(1, SLABS, push, 0)

    def push_coil(t, part, landing, ssem, rsem):
        def push(k, carry):
            to = lax.rem(mg + k, GROUPS)
            pltpu.make_async_remote_copy(
                src_ref=part.at[t, to], dst_ref=landing.at[t, mg],
                send_sem=ssem.at[t], recv_sem=rsem.at[t],
                device_id=(me, to), device_id_type=MESH,
            ).start()
            return carry

        lax.fori_loop(1, GROUPS, push, 0)

    def push_sum(t, total, ssem, rsem):
        def push(k, carry):
            to = lax.rem(mg + k, GROUPS)
            pltpu.make_async_remote_copy(
                src_ref=total.at[t, mg], dst_ref=total.at[t, mg],
                send_sem=ssem.at[t], recv_sem=rsem.at[t],
                device_id=(me, to), device_id_type=MESH,
            ).start()
            return carry

        lax.fori_loop(1, GROUPS, push, 0)

    def drain(buffer, t, count, sem):
        view = buffer.at[t, pl.ds(0, count)]
        pltpu.make_async_copy(view, view, sem.at[t]).wait()

    def finish_sum(t, part, landing, total, rsem, ssem2, rsem2):
        drain(landing, t, GROUPS - 1, rsem)
        landing[t, mg] = part[t, mg]
        value = landing[t, 0].astype(F32)
        for j in range(1, GROUPS):
            value = value + landing[t, j].astype(F32)
        total[t, mg] = value.astype(BF16)
        push_sum(t, total, ssem2, rsem2)

    data_chunk(0)
    pl.semaphore_wait(barrier, SLABS - 1 + GROUPS - 1)
    push_data(0)

    def push_mask(k, carry):
        to = lax.rem(me + k, SLABS)
        pltpu.make_async_remote_copy(
            src_ref=own_mask, dst_ref=all_mask.at[me],
            send_sem=mask_send, recv_sem=mask_recv,
            device_id=(to, mg), device_id_type=MESH,
        ).start()
        return carry

    lax.fori_loop(1, SLABS, push_mask, 0)

    loads[2].wait()
    row, col = iotas(2 * N, 2 * N)
    untie = as_bf16(col == 2 * (row % N) + row // N)
    for x in range(LOCAL):
        pair = dot(untie, lanes([coef[0, x], coef[1, x]]))
        for t in range(PTS):
            re = im = None
            for l in range(2):
                where = (2 * mg + l) * PTS + t
                b_re, b_im = basis[where], basis[16 * PTS + where]
                x_re = pair[:N, l * N : (l + 1) * N]
                x_im = pair[N:, l * N : (l + 1) * N]
                r, i = b_re * x_re - b_im * x_im, b_re * x_im + b_im * x_re
                re, im = (r, i) if re is None else (re + r, im + i)
            image_part[t, :, 0, x] = re.astype(BF16).reshape(GROUPS, ROWS, N)
            image_part[t, :, 1, x] = im.astype(BF16).reshape(GROUPS, ROWS, N)
    for t in range(PTS):
        push_coil(t, image_part, image_recv, irs_send, irs_recv)

    def later_chunk(t, carry):
        data_chunk(t)
        push_data(t)
        return carry

    lax.fori_loop(1, PTS, later_chunk, 0)

    loads[3].wait()
    for x in range(LOCAL):
        both = dot(untie, lanes([maps[c, x] for c in range(LOCAL)]))
        sens_re[x] = both[:N]
        sens_im[x] = both[N:]
    for t in range(PTS):
        finish_sum(t, image_part, image_recv, image_all, irs_recv, iag_send, iag_recv)
    loads[4].wait()
    for x in range(LOCAL):
        angle = (field[x] & (STEPS_CYCLE - 1)).astype(F32) * (2.0 * math.pi / STEPS_CYCLE)
        c1, s1 = jnp.cos(angle), jnp.sin(angle)
        c2, s2 = c1 * c1 - s1 * s1, 2.0 * (c1 * s1)
        c3, s3 = c2 * c1 - s2 * s1, s2 * c1 + c2 * s1
        c4, s4 = c2 * c2 - s2 * s2, 2.0 * (c2 * s2)
        for t, (c, s) in enumerate([(c1, s1), (c2, s2), (c3, s3), (c4, s4)]):
            cosine[t, x] = c
            sine[t, x] = s
    row, col = iotas(2 * N, 8 * N)
    spread = as_bf16(
        (row // N == col // (4 * N)) & (row % N == 4 * ((col % (4 * N)) // 16) + col % 4)
    )
    wide = dot(table[0], spread)
    for x in range(LOCAL):
        mix_y[x] = jnp.where((col // 4) % 4 == x, wide, 0.0).astype(BF16)

    mask_view = all_mask.at[pl.ds(0, SLABS - 1)]
    pltpu.make_async_copy(mask_view, mask_view, mask_recv).wait()
    all_mask[me] = own_mask[...]
    row, col = iotas(N, SLABS * 16)
    everything = all_mask[...].reshape(SLABS * 16, N)
    for t in range(PTS):
        pick = as_bf16((col // 16 == row // 4) & (col % 4 == row % 4) & ((col // 4) % 4 == t))
        mask_full[t] = dot(pick, everything)

    def model_term(t):
        drain(image_all, t, GROUPS - 1, iag_recv)

        def one(x, carry):
            i_re = image_all[t, :, 0, x].reshape(N, N).astype(F32)
            i_im = image_all[t, :, 1, x].reshape(N, N).astype(F32)
            c, s = cosine[t, x], sine[t, x]
            t_re, t_im = c * i_re - s * i_im, s * i_re + c * i_im
            s_re, s_im = sens_re[x], sens_im[x]
            stack = []
            for k in range(LOCAL):
                a, b = s_re[:, k * N : (k + 1) * N], s_im[:, k * N : (k + 1) * N]
                stack.append(lanes([(a * t_re - b * t_im).astype(BF16), (a * t_im + b * t_re).astype(BF16)]))
            depth = dot(rows_of(stack), table[0]).astype(BF16)
            planes = rows_of(
                [lanes([depth[k * N : (k + 1) * N, p * N : (p + 1) * N] for k in range(LOCAL)]) for p in range(2)]
            )
            lines = dot(table[1], planes)
            m = lanes([mask_full[t]] * LOCAL)
            lines = rows_of([(lines[:N] * m).astype(BF16), (lines[N:] * m).astype(BF16)])
            back = dot(table[0], lines).astype(BF16)
            stack = rows_of(
                [lanes([back[p * N : (p + 1) * N, k * N : (k + 1) * N] for p in range(2)]) for k in range(LOCAL)]
            )
            back = dot(stack, table[1])
            q_re = q_im = None
            for k in range(LOCAL):
                a, b = s_re[:, k * N : (k + 1) * N], s_im[:, k * N : (k + 1) * N]
                r, i = back[k * N : (k + 1) * N, :N], back[k * N : (k + 1) * N, N:]
                u, v = a * r + b * i, a * i - b * r
                q_re, q_im = (u, v) if q_re is None else (q_re + u, q_im + v)
            model[t, x, 0] = q_re
            model[t, x, 1] = q_im
            return carry

        lax.fori_loop(0, LOCAL, one, 0)

    def model_step(t, carry):
        model_term(t)
        return carry

    lax.fori_loop(0, PTS, model_step, 0)

    def data_term(t):
        drain(recv, t, SLABS - 1, recv_sem)
        self_copy(t).wait()

        def one(x, carry):
            arrived = recv[t].reshape(SLABS * 16, 2 * LOCAL * N)
            mix = mix_y[x]
            plane = dot(mix[:, : 4 * N], arrived[:, : 4 * N]) + dot(mix[:, 4 * N :], arrived[:, 4 * N :])
            s_re, s_im = sens_re[x], sens_im[x]
            r, i = plane[:N], plane[N:]
            u, v = s_re * r + s_im * i, s_re * i - s_im * r
            q_re, q_im = model[t, x, 0], model[t, x, 1]
            for k in range(LOCAL):
                q_re = q_re - u[:, k * N : (k + 1) * N]
                q_im = q_im - v[:, k * N : (k + 1) * N]
            comb_part[t, :, 0, x] = q_re.astype(BF16).reshape(GROUPS, ROWS, N)
            comb_part[t, :, 1, x] = q_im.astype(BF16).reshape(GROUPS, ROWS, N)
            return carry

        lax.fori_loop(0, LOCAL, one, 0)
        push_coil(t, comb_part, comb_recv, crs_send, crs_recv)

    def accumulate(t):
        drain(comb_all, t, GROUPS - 1, cag_recv)
        for x in range(LOCAL):
            q_re = comb_all[t, :, 0, x].reshape(N, N).astype(F32)
            q_im = comb_all[t, :, 1, x].reshape(N, N).astype(F32)
            c, s = cosine[t, x], sine[t, x]
            w_re, w_im = c * q_re + s * q_im, c * q_im - s * q_re
            for l in range(2):
                where = (2 * mg + l) * PTS + t
                b_re, b_im = basis[where], basis[16 * PTS + where]
                g_re, g_im = b_re * w_re + b_im * w_im, b_re * w_im - b_im * w_re
                if t:
                    g_re = g_re + grad[l, x, 0]
                    g_im = g_im + grad[l, x, 1]
                if t < PTS - 1:
                    grad[l, x, 0] = g_re
                    grad[l, x, 1] = g_im
                else:
                    out_ref[l, x, pl.ds(0, N, stride=2), :] = g_re
                    out_ref[l, x, pl.ds(1, N, stride=2), :] = g_im

    finish = functools.partial(
        finish_sum, part=comb_part, landing=comb_recv, total=comb_all, rsem=crs_recv, ssem2=cag_send, rsem2=cag_recv
    )
    for t in range(PTS):
        data_term(t)
        if t >= 1:
            finish(t - 1)
        if t >= 2:
            accumulate(t - 2)
    finish(PTS - 1)
    accumulate(PTS - 2)
    accumulate(PTS - 1)

    def spent(k, carry):
        drain(send, k, SLABS - 1, send_sem)
        drain(image_part, k, GROUPS - 1, irs_send)
        drain(image_part, k, GROUPS - 1, iag_send)
        drain(comb_part, k, GROUPS - 1, crs_send)
        drain(comb_part, k, GROUPS - 1, cag_send)
        return carry

    lax.fori_loop(0, PTS, spent, 0)
    pltpu.make_async_copy(mask_view, mask_view, mask_send).wait()


def step(coef, basis, maps, field, data, mask):
    any_space = pl.BlockSpec(memory_space=pl.ANY)
    shared = (PTS, GROUPS, 2, LOCAL, ROWS, N)
    dma = pltpu.SemaphoreType.DMA
    scratch = [
        pltpu.VMEM((2, LOCAL, 2 * N, N), BF16),
        pltpu.VMEM((LOCAL, LOCAL, 2 * N, N), BF16),
        pltpu.VMEM((LOCAL, N, N), I32),
        pltpu.VMEM((PTS, 4, N), I32),
        pltpu.VMEM((2, 2 * N, 2 * N), BF16),
        pltpu.VMEM((PTS, 8 * N, LOCAL * N), BF16),
        pltpu.VMEM((8 * N, 8 * N), BF16),
        pltpu.VMEM((LOCAL, 2 * N, 8 * N), BF16),
        pltpu.VMEM((PTS, SLABS, 16, 2 * LOCAL * N), BF16),
        pltpu.VMEM((PTS, SLABS, 16, 2 * LOCAL * N), BF16),
        pltpu.VMEM((16, N), BF16),
        pltpu.VMEM((SLABS, 16, N), BF16),
        pltpu.VMEM((PTS, N, N), F32),
        pltpu.VMEM((LOCAL, N, LOCAL * N), F32),
        pltpu.VMEM((LOCAL, N, LOCAL * N), F32),
        pltpu.VMEM((PTS, LOCAL, N, N), F32),
        pltpu.VMEM((PTS, LOCAL, N, N), F32),
        pltpu.VMEM(shared, BF16),
        pltpu.VMEM(shared, BF16),
        pltpu.VMEM(shared, BF16),
        pltpu.VMEM((PTS, LOCAL, 2, N, N), F32),
        pltpu.VMEM(shared, BF16),
        pltpu.VMEM(shared, BF16),
        pltpu.VMEM(shared, BF16),
        pltpu.VMEM((2, LOCAL, 2, N, N), F32),
        dma((5,)), dma((PTS, LOCAL)), dma((PTS,)), dma((PTS,)), dma((PTS,)), dma, dma,
        dma((PTS,)), dma((PTS,)), dma((PTS,)), dma((PTS,)),
        dma((PTS,)), dma((PTS,)), dma((PTS,)), dma((PTS,)),
    ]
    out = pl.pallas_call(
        body,
        out_shape=jax.ShapeDtypeStruct((2, LOCAL, 2 * N, N), F32),
        in_specs=[any_space, pl.BlockSpec(memory_space=pltpu.SMEM)] + [any_space] * 5,
        out_specs=pl.BlockSpec(memory_space=pltpu.VMEM),
        scratch_shapes=scratch,
        compiler_params=pltpu.CompilerParams(
            collective_id=0, has_side_effects=True, vmem_limit_bytes=56 << 20
        ),
    )(
        coef.reshape(2, LOCAL, 2 * N, N),
        basis.astype(F32).reshape(-1),
        maps.reshape(LOCAL, LOCAL, 2 * N, N),
        field,
        data.reshape(LOCAL, PTS, 8 * N, N),
        mask,
        jnp.asarray(dft_pair()),
    )
    return out.reshape(2, LOCAL, N, 2, N)


def solution(mesh):
    in_specs = (
        P("coil", "space", None, None, None),
        P(),
        P("coil", "space", None, None, None),
        P("space", None, None),
        P("coil", None, None, "space", None, None),
        P(None, "space", None),
    )
    out_specs = P("coil", "space", None, None, None)
    return jax.shard_map(step, mesh=mesh, in_specs=in_specs, out_specs=out_specs, check_vma=False)
```

```python
import math

import jax
import jax.numpy as jnp
import numpy as np
from jax import lax
from jax.experimental import pallas as pl
from jax.experimental.pallas import tpu as pltpu
from jax.sharding import PartitionSpec as P

STEPS_CYCLE = 256
N = 128
PTS = 4
LOCAL = 4
SLABS = 32
GROUPS = 8
RING = 4
QUARTER = N // RING
PIECES = 2 * PTS
F32 = jnp.float32
BF16 = jnp.bfloat16
I32 = jnp.int32
MESH = pl.DeviceIdType.MESH


def dft_pair():
    index = np.arange(N)
    angle = (index[:, None] * index[None, :] % N).astype(np.float32) * np.float32(2.0 * math.pi / N)
    cosine = np.cos(angle) / np.float32(math.sqrt(N))
    sine = np.sin(angle) / np.float32(math.sqrt(N))
    inverse = np.block([[cosine, -sine], [sine, cosine]])
    return np.stack([inverse, inverse.T]).astype(jnp.bfloat16)


def dot(a, b):
    return jnp.dot(a, b, preferred_element_type=F32)


def iotas(rows, cols):
    return (
        lax.broadcasted_iota(I32, (rows, cols), 0),
        lax.broadcasted_iota(I32, (rows, cols), 1),
    )


def as_bf16(condition):
    return jnp.where(condition, 1.0, 0.0).astype(BF16)


def lanes(parts):
    return jnp.concatenate(parts, axis=1)


def rows_of(parts):
    return jnp.concatenate(parts, axis=0)


def body(
    coef_hbm, basis_hbm, maps_hbm, field_hbm, data_hbm, mask_hbm, table_hbm, out_ref,
    coef, basis, maps, field, mask, table, data, mix_x, mix_y, send, recv, own_mask, all_mask, mask_full,
    sens_re, sens_im, cosine, sine, weight, model, grad,
    image_part, image_land, image_half, image_all, comb_part, comb_land, comb_half, comb_all,
    load_sem, data_sem, self_sem, send_sem, recv_sem, mask_send, mask_recv, image_sem, comb_sem,
):
    me = lax.axis_index("space")
    mg = lax.axis_index("coil")
    side = mg // RING
    place = lax.rem(mg, RING)

    barrier = pltpu.get_barrier_semaphore()

    def greet_space(k, carry):
        pl.semaphore_signal(barrier, inc=1, device_id=(lax.rem(me + k, SLABS), mg), device_id_type=MESH)
        return carry

    def greet_coil(k, carry):
        pl.semaphore_signal(barrier, inc=1, device_id=(me, lax.rem(mg + k, GROUPS)), device_id_type=MESH)
        return carry

    lax.fori_loop(1, SLABS, greet_space, 0)
    lax.fori_loop(1, GROUPS, greet_coil, 0)

    loads = [
        pltpu.make_async_copy(src, dst, load_sem.at[i])
        for i, (src, dst) in enumerate(
            [
                (table_hbm, table), (mask_hbm, mask), (coef_hbm, coef),
                (maps_hbm, maps), (field_hbm, field), (basis_hbm, basis),
            ]
        )
    ]

    def data_load(t, c):
        return pltpu.make_async_copy(
            data_hbm.at[c, t], data.at[t, :, pl.ds(c * N, N)], data_sem.at[t, c]
        )

    loads[0].start()
    loads[1].start()
    for c in range(LOCAL):
        data_load(0, c).start()
    for load in loads[2:]:
        load.start()
    for t in range(1, PTS):
        for c in range(LOCAL):
            data_load(t, c).start()
    loads[0].wait()

    row, col = iotas(2 * N, 8 * N)
    spread = as_bf16((row % N == col // 8) & (row // N == col % 2))
    wide = dot(table[0], spread).astype(BF16)
    row, col = iotas(2 * N, N // 2)
    repeat = as_bf16(col == row // 4)
    row, col = iotas(2 * N, 8 * N)
    same_line = row % 4 == (col // 2) % 4
    for block in range(4):
        part = dot(repeat, wide[block * (N // 2) : (block + 1) * (N // 2)])
        mix_x[pl.ds(block * 2 * N, 2 * N), :] = jnp.where(same_line, part, 0.0).astype(BF16)
    loads[1].wait()
    for t in range(PTS):
        own_mask[pl.ds(t * 4, 4), :] = mask[t].astype(F32).astype(BF16)

    def data_chunk(t):
        for c in range(LOCAL):
            data_load(t, c).wait()
        lines = mask[t].astype(F32)
        lines = rows_of([lines, lines])
        lines = lanes([lines] * LOCAL)
        for half in range(2):
            parts = []
            for p in range(2):
                mixed = dot(mix_x[pl.ds((2 * p + half) * 2 * N, 2 * N), :], data[t])
                mixed = mixed.reshape(32, 8, LOCAL * N) * lines[None]
                parts.append(mixed.reshape(2 * N, LOCAL * N).astype(BF16))
            stacked = rows_of(
                [lanes([parts[0][:, c * N : (c + 1) * N], parts[1][:, c * N : (c + 1) * N]]) for c in range(LOCAL)]
            )
            turned = dot(stacked, table[1])
            for h in range(2):
                for p in range(2):
                    for low in range(2):
                        piece = jnp.concatenate(
                            [
                                turned[c * 2 * N : (c + 1) * 2 * N, p * N : (p + 1) * N].reshape(16, 2, 8, N)[:, h]
                                for c in (low, 2 + low)
                            ],
                            axis=1,
                        )
                        send[t, pl.ds(half * 16, 16), h, :, pl.ds((2 * p + low) * N, N)] = piece.astype(BF16)

    def self_copy(t, h):
        return pltpu.make_async_copy(send.at[t, me, h], recv.at[t, me, h], self_sem.at[2 * t + h])

    def push_data(t):
        for h in range(2):
            self_copy(t, h).start()

            def push(k, carry):
                to = lax.rem(me + k, SLABS)
                pltpu.make_async_remote_copy(
                    src_ref=send.at[t, to, h], dst_ref=recv.at[t, me, h],
                    send_sem=send_sem.at[2 * t + h], recv_sem=recv_sem.at[2 * t + h],
                    device_id=(to, mg), device_id_type=MESH,
                ).start()
                return carry

            lax.fori_loop(1, SLABS, push, 0)

    def drain(view, sem):
        pltpu.make_async_copy(view, view, sem).wait()

    def to_ring(source, target, ssem, rsem):
        for k in (2, 1, 3):
            to = lax.rem(place + k, RING)
            pltpu.make_async_remote_copy(
                src_ref=source(to), dst_ref=target, send_sem=ssem, recv_sem=rsem,
                device_id=(me, side * RING + to), device_id_type=MESH,
            ).start()

    def ring_start(part, land, sem):
        to_ring(lambda to: part.at[to], land.at[place], sem.at[0], sem.at[1])

    def ring_sum(part, land, half, sem, lead):
        drain(land.at[pl.ds(0, RING - 1)], sem.at[1])

        def one(i, carry):
            land[place, i] = part[place, i]
            value = land[0, i].astype(F32)
            for j in range(1, RING):
                value = value + land[j, i].astype(F32)
            half[0, i] = value.astype(BF16)
            return carry

        lax.fori_loop(0, lead, one, 0)
        pltpu.make_async_remote_copy(
            src_ref=half.at[0], dst_ref=half.at[1], send_sem=sem.at[2], recv_sem=sem.at[3],
            device_id=(me, (1 - side) * RING + place), device_id_type=MESH,
        ).start()

    def pair_sum(half, total, sem, lead):
        drain(half.at[1], sem.at[3])

        def one(i, carry):
            total[place, i] = (half[0, i].astype(F32) + half[1, i].astype(F32)).astype(BF16)
            return carry

        lax.fori_loop(0, lead, one, 0)
        to_ring(lambda to: total.at[place], total.at[place], sem.at[4], sem.at[5])

    def ring_end(total, sem):
        drain(total.at[pl.ds(0, RING - 1)], sem.at[5])

    def ring_spent(part, half, total, sem):
        drain(part.at[pl.ds(0, RING - 1)], sem.at[0])
        drain(half.at[0], sem.at[2])
        drain(total.at[pl.ds(0, RING - 1)], sem.at[4])

    data_chunk(0)
    pl.semaphore_wait(barrier, SLABS - 1 + GROUPS - 1)
    push_data(0)

    def push_mask(k, carry):
        to = lax.rem(me + k, SLABS)
        pltpu.make_async_remote_copy(
            src_ref=own_mask, dst_ref=all_mask.at[me],
            send_sem=mask_send, recv_sem=mask_recv,
            device_id=(to, mg), device_id_type=MESH,
        ).start()
        return carry

    lax.fori_loop(1, SLABS, push_mask, 0)

    def later_chunk(t, carry):
        data_chunk(t)
        push_data(t)
        return carry

    lax.fori_loop(1, PTS, later_chunk, 0)

    loads[5].wait()
    rows = basis[...].astype(F32).reshape(2 * PTS, 4 * PTS)
    _, col = iotas(2 * PTS, 4 * PTS)
    for l in range(2):
        mine = jnp.sum(jnp.where(col == 2 * mg + l, rows, 0.0), axis=1, keepdims=True)
        weight[l] = jnp.broadcast_to(mine, (2 * PTS, N))
    loads[2].wait()
    row, col = iotas(2 * N, 2 * N)
    untie = as_bf16(col == 2 * (row % N) + row // N)
    for x in range(LOCAL):
        pair = dot(untie, lanes([coef[0, x], coef[1, x]]))
        for t in range(PTS):
            re = im = None
            for l in range(2):
                b_re, b_im = weight[l, pl.ds(t, 1)], weight[l, pl.ds(PTS + t, 1)]
                x_re = pair[:N, l * N : (l + 1) * N]
                x_im = pair[N:, l * N : (l + 1) * N]
                r, i = b_re * x_re - b_im * x_im, b_re * x_im + b_im * x_re
                re, im = (r, i) if re is None else (re + r, im + i)
            image_part[:, t, 0, x] = re.astype(BF16).reshape(RING, QUARTER, N)
            image_part[:, t, 1, x] = im.astype(BF16).reshape(RING, QUARTER, N)
    ring_start(image_part, image_land, image_sem)

    loads[3].wait()
    for x in range(LOCAL):
        both = dot(untie, lanes([maps[c, x] for c in range(LOCAL)]))
        sens_re[x] = both[:N]
        sens_im[x] = both[N:]
    ring_sum(image_part, image_land, image_half, image_sem, PTS)
    loads[4].wait()
    for x in range(LOCAL):
        angle = (field[x] & (STEPS_CYCLE - 1)).astype(F32) * (2.0 * math.pi / STEPS_CYCLE)
        c1, s1 = jnp.cos(angle), jnp.sin(angle)
        c2, s2 = c1 * c1 - s1 * s1, 2.0 * (c1 * s1)
        c3, s3 = c2 * c1 - s2 * s1, s2 * c1 + c2 * s1
        c4, s4 = c2 * c2 - s2 * s2, 2.0 * (c2 * s2)
        for t, (c, s) in enumerate([(c1, s1), (c2, s2), (c3, s3), (c4, s4)]):
            cosine[t, x] = c
            sine[t, x] = s
    pair_sum(image_half, image_all, image_sem, PTS)
    row, col = iotas(2 * N, 8 * N)
    spread = as_bf16(
        (row // N == col // (4 * N)) & (row % N == 4 * ((col % (4 * N)) // 16) + col % 4)
    )
    wide = dot(table[0], spread)
    for j in range(4):
        mix_y[j] = jnp.where((col // 4) % 4 == j, wide, 0.0).astype(BF16)

    mask_view = all_mask.at[pl.ds(0, SLABS - 1)]
    pltpu.make_async_copy(mask_view, mask_view, mask_recv).wait()
    all_mask[me] = own_mask[...]
    row, col = iotas(N, SLABS * 16)
    everything = all_mask[...].reshape(SLABS * 16, N)
    for t in range(PTS):
        pick = as_bf16((col // 16 == row // 4) & (col % 4 == row % 4) & ((col // 4) % 4 == t))
        mask_full[t] = dot(pick, everything)

    def model_term(t):
        def one(x, carry):
            i_re = image_all[:, t, 0, x].reshape(N, N).astype(F32)
            i_im = image_all[:, t, 1, x].reshape(N, N).astype(F32)
            c, s = cosine[t, x], sine[t, x]
            t_re, t_im = c * i_re - s * i_im, s * i_re + c * i_im
            s_re, s_im = sens_re[x], sens_im[x]
            stack = []
            for k in range(LOCAL):
                a, b = s_re[:, k * N : (k + 1) * N], s_im[:, k * N : (k + 1) * N]
                stack.append(lanes([(a * t_re - b * t_im).astype(BF16), (a * t_im + b * t_re).astype(BF16)]))
            depth = dot(rows_of(stack), table[0]).astype(BF16)
            planes = rows_of(
                [lanes([depth[k * N : (k + 1) * N, p * N : (p + 1) * N] for k in range(LOCAL)]) for p in range(2)]
            )
            lines = dot(table[1], planes)
            m = lanes([mask_full[t]] * LOCAL)
            lines = rows_of([(lines[:N] * m).astype(BF16), (lines[N:] * m).astype(BF16)])
            back = dot(table[0], lines).astype(BF16)
            stack = rows_of(
                [lanes([back[p * N : (p + 1) * N, k * N : (k + 1) * N] for p in range(2)]) for k in range(LOCAL)]
            )
            back = dot(stack, table[1])
            q_re = q_im = None
            for k in range(LOCAL):
                a, b = s_re[:, k * N : (k + 1) * N], s_im[:, k * N : (k + 1) * N]
                r, i = back[k * N : (k + 1) * N, :N], back[k * N : (k + 1) * N, N:]
                u, v = a * r + b * i, a * i - b * r
                q_re, q_im = (u, v) if q_re is None else (q_re + u, q_im + v)
            model[t, x, 0] = q_re
            model[t, x, 1] = q_im
            return carry

        lax.fori_loop(0, LOCAL, one, 0)

    def model_step(t, carry):
        model_term(t)
        return carry

    ring_end(image_all, image_sem)
    lax.fori_loop(0, PTS, model_step, 0)

    def data_term(n):
        t, h = n // 2, lax.rem(n, 2)
        drain(recv.at[t, pl.ds(0, SLABS - 1), h], recv_sem.at[n])
        self_copy(t, h).wait()

        def one(j, carry):
            x = 2 * h + j
            arrived = recv[t, :, h].reshape(SLABS * 16, 4 * N)
            q_re, q_im = model[t, x, 0], model[t, x, 1]
            for high in range(2):
                mix = mix_y[2 * high + j]
                plane = dot(mix[:, : 4 * N], arrived[:, : 2 * N]) + dot(mix[:, 4 * N :], arrived[:, 2 * N :])
                s_re = sens_re[x, :, pl.ds(high * 2 * N, 2 * N)]
                s_im = sens_im[x, :, pl.ds(high * 2 * N, 2 * N)]
                r, i = plane[:N], plane[N:]
                u, v = s_re * r + s_im * i, s_re * i - s_im * r
                q_re = q_re - u[:, :N] - u[:, N:]
                q_im = q_im - v[:, :N] - v[:, N:]
            comb_part[n, :, 0, j] = q_re.astype(BF16).reshape(RING, QUARTER, N)
            comb_part[n, :, 1, j] = q_im.astype(BF16).reshape(RING, QUARTER, N)
            return carry

        lax.fori_loop(0, 2, one, 0)
        ring_start(comb_part.at[n], comb_land.at[n], comb_sem.at[n])

    def middle(n):
        ring_sum(comb_part.at[n], comb_land.at[n], comb_half.at[n], comb_sem.at[n], 2)

    def last(n):
        pair_sum(comb_half.at[n], comb_all.at[n], comb_sem.at[n], 2)

    def accumulate(n, final):
        t, h = n // 2, n % 2 if final else lax.rem(n, 2)
        ring_end(comb_all.at[n], comb_sem.at[n])
        for j in range(2):
            x = 2 * h + j
            q_re = comb_all[n, :, 0, j].reshape(N, N).astype(F32)
            q_im = comb_all[n, :, 1, j].reshape(N, N).astype(F32)
            c, s = cosine[t, x], sine[t, x]
            w_re, w_im = c * q_re + s * q_im, c * q_im - s * q_re
            for l in range(2):
                b_re, b_im = weight[l, pl.ds(t, 1)], weight[l, pl.ds(PTS + t, 1)]
                g_re = grad[l, x, 0] + (b_re * w_re + b_im * w_im)
                g_im = grad[l, x, 1] + (b_re * w_im - b_im * w_re)
                if final:
                    out_ref[l, x, pl.ds(0, N, stride=2), :] = g_re
                    out_ref[l, x, pl.ds(1, N, stride=2), :] = g_im
                else:
                    grad[l, x, 0] = g_re
                    grad[l, x, 1] = g_im

    grad[...] = jnp.zeros(grad.shape, F32)

    def piece_step(n, carry):
        data_term(n)

        @pl.when(n >= 1)
        def _():
            middle(n - 1)

        @pl.when(n >= 2)
        def _():
            accumulate(n - 2, False)

        @pl.when(n >= 1)
        def _():
            last(n - 1)

        return carry

    lax.fori_loop(0, PIECES, piece_step, 0)
    middle(PIECES - 1)
    accumulate(PIECES - 2, True)
    last(PIECES - 1)
    accumulate(PIECES - 1, True)

    def spent(n, carry):
        drain(send.at[n // 2, pl.ds(0, SLABS - 1), lax.rem(n, 2)], send_sem.at[n])
        ring_spent(comb_part.at[n], comb_half.at[n], comb_all.at[n], comb_sem.at[n])
        return carry

    lax.fori_loop(0, PIECES, spent, 0)
    ring_spent(image_part, image_half, image_all, image_sem)
    pltpu.make_async_copy(mask_view, mask_view, mask_send).wait()


def step(coef, basis, maps, field, data, mask):
    any_space = pl.BlockSpec(memory_space=pl.ANY)
    dma = pltpu.SemaphoreType.DMA
    image = (PTS, 2, LOCAL, QUARTER, N)
    comb = (2, 2, QUARTER, N)
    scratch = [
        pltpu.VMEM((2, LOCAL, 2 * N, N), BF16),
        pltpu.VMEM((2, PTS, 4 * PTS), BF16),
        pltpu.VMEM((LOCAL, LOCAL, 2 * N, N), BF16),
        pltpu.VMEM((LOCAL, N, N), I32),
        pltpu.VMEM((PTS, 4, N), I32),
        pltpu.VMEM((2, 2 * N, 2 * N), BF16),
        pltpu.VMEM((PTS, 8 * N, LOCAL * N), BF16),
        pltpu.VMEM((8 * N, 8 * N), BF16),
        pltpu.VMEM((4, 2 * N, 8 * N), BF16),
        pltpu.VMEM((PTS, SLABS, 2, 16, 4 * N), BF16),
        pltpu.VMEM((PTS, SLABS, 2, 16, 4 * N), BF16),
        pltpu.VMEM((16, N), BF16),
        pltpu.VMEM((SLABS, 16, N), BF16),
        pltpu.VMEM((PTS, N, N), F32),
        pltpu.VMEM((LOCAL, N, LOCAL * N), F32),
        pltpu.VMEM((LOCAL, N, LOCAL * N), F32),
        pltpu.VMEM((PTS, LOCAL, N, N), F32),
        pltpu.VMEM((PTS, LOCAL, N, N), F32),
        pltpu.VMEM((2, 2 * PTS, N), F32),
        pltpu.VMEM((PTS, LOCAL, 2, N, N), F32),
        pltpu.VMEM((2, LOCAL, 2, N, N), F32),
        pltpu.VMEM((RING,) + image, BF16),
        pltpu.VMEM((RING,) + image, BF16),
        pltpu.VMEM((2,) + image, BF16),
        pltpu.VMEM((RING,) + image, BF16),
        pltpu.VMEM((PIECES, RING) + comb, BF16),
        pltpu.VMEM((PIECES, RING) + comb, BF16),
        pltpu.VMEM((PIECES, 2) + comb, BF16),
        pltpu.VMEM((PIECES, RING) + comb, BF16),
        dma((6,)), dma((PTS, LOCAL)), dma((PIECES,)), dma((PIECES,)), dma((PIECES,)), dma, dma,
        dma((6,)), dma((PIECES, 6)),
    ]
    out = pl.pallas_call(
        body,
        out_shape=jax.ShapeDtypeStruct((2, LOCAL, 2 * N, N), F32),
        in_specs=[any_space] * 7,
        out_specs=pl.BlockSpec(memory_space=pltpu.VMEM),
        scratch_shapes=scratch,
        compiler_params=pltpu.CompilerParams(
            collective_id=0, has_side_effects=True, vmem_limit_bytes=56 << 20
        ),
    )(
        coef.reshape(2, LOCAL, 2 * N, N),
        jnp.transpose(basis, (0, 2, 1)),
        maps.reshape(LOCAL, LOCAL, 2 * N, N),
        field,
        data.reshape(LOCAL, PTS, 8 * N, N),
        mask,
        jnp.asarray(dft_pair()),
    )
    return out.reshape(2, LOCAL, N, 2, N)


def solution(mesh):
    in_specs = (
        P("coil", "space", None, None, None),
        P(),
        P("coil", "space", None, None, None),
        P("space", None, None),
        P("coil", None, None, "space", None, None),
        P(None, "space", None),
    )
    out_specs = P("coil", "space", None, None, None)
    return jax.shard_map(step, mesh=mesh, in_specs=in_specs, out_specs=out_specs, check_vma=False)
```

```python
import math

import jax
import jax.numpy as jnp
import numpy as np
from jax import lax
from jax.experimental import pallas as pl
from jax.experimental.pallas import tpu as pltpu
from jax.sharding import PartitionSpec as P

STEPS_CYCLE = 256
N = 128
PTS = 4
LOCAL = 4
SLABS = 32
GROUPS = 8
RING = 4
QUARTER = N // RING
ROWS = N // GROUPS
PIECES = 2 * PTS
F32 = jnp.float32
BF16 = jnp.bfloat16
I32 = jnp.int32
MESH = pl.DeviceIdType.MESH


def dft_pair():
    index = np.arange(N)
    angle = (index[:, None] * index[None, :] % N).astype(np.float32) * np.float32(2.0 * math.pi / N)
    cosine = np.cos(angle) / np.float32(math.sqrt(N))
    sine = np.sin(angle) / np.float32(math.sqrt(N))
    inverse = np.block([[cosine, -sine], [sine, cosine]])
    return np.stack([inverse, inverse.T]).astype(jnp.bfloat16)


def dot(a, b):
    return jnp.dot(a, b, preferred_element_type=F32)


def iotas(rows, cols):
    return (
        lax.broadcasted_iota(I32, (rows, cols), 0),
        lax.broadcasted_iota(I32, (rows, cols), 1),
    )


def as_bf16(condition):
    return jnp.where(condition, 1.0, 0.0).astype(BF16)


def lanes(parts):
    return jnp.concatenate(parts, axis=1)


def rows_of(parts):
    return jnp.concatenate(parts, axis=0)


def body(
    coef_hbm, basis_hbm, maps_hbm, field_hbm, data_hbm, mask_hbm, table_hbm, out_ref,
    coef, basis, maps, field, mask, table, data, mix_x, mix_y, send, recv, own_mask, all_mask, mask_full,
    sens_re, sens_im, cosine, sine, weight, model, grad,
    image_part, image_land, image_half, image_all, comb_part, comb_land, comb_half, comb_all, end_land,
    load_sem, data_sem, self_sem, send_sem, recv_sem, mask_send, mask_recv, image_sem, comb_sem, end_sem,
):
    me = lax.axis_index("space")
    mg = lax.axis_index("coil")
    side = mg // RING
    place = lax.rem(mg, RING)

    barrier = pltpu.get_barrier_semaphore()

    def greet_space(k, carry):
        pl.semaphore_signal(barrier, inc=1, device_id=(lax.rem(me + k, SLABS), mg), device_id_type=MESH)
        return carry

    def greet_coil(k, carry):
        pl.semaphore_signal(barrier, inc=1, device_id=(me, lax.rem(mg + k, GROUPS)), device_id_type=MESH)
        return carry

    lax.fori_loop(1, SLABS, greet_space, 0)
    lax.fori_loop(1, GROUPS, greet_coil, 0)

    loads = [
        pltpu.make_async_copy(src, dst, load_sem.at[i])
        for i, (src, dst) in enumerate(
            [
                (table_hbm, table), (mask_hbm, mask), (coef_hbm, coef),
                (maps_hbm, maps), (field_hbm, field), (basis_hbm, basis),
            ]
        )
    ]

    def data_load(t, c):
        return pltpu.make_async_copy(
            data_hbm.at[c, t], data.at[t, :, pl.ds(c * N, N)], data_sem.at[t, c]
        )

    loads[0].start()
    loads[1].start()
    for c in range(LOCAL):
        data_load(0, c).start()
    for load in loads[2:]:
        load.start()
    for t in range(1, PTS):
        for c in range(LOCAL):
            data_load(t, c).start()
    loads[0].wait()

    row, col = iotas(2 * N, 8 * N)
    spread = as_bf16((row % N == col // 8) & (row // N == col % 2))
    wide = dot(table[0], spread).astype(BF16)
    row, col = iotas(2 * N, N // 2)
    repeat = as_bf16(col == row // 4)
    row, col = iotas(2 * N, 8 * N)
    same_line = row % 4 == (col // 2) % 4
    for block in range(4):
        part = dot(repeat, wide[block * (N // 2) : (block + 1) * (N // 2)])
        mix_x[pl.ds(block * 2 * N, 2 * N), :] = jnp.where(same_line, part, 0.0).astype(BF16)
    loads[1].wait()
    for t in range(PTS):
        own_mask[pl.ds(t * 4, 4), :] = mask[t].astype(F32).astype(BF16)

    def data_chunk(t):
        for c in range(LOCAL):
            data_load(t, c).wait()
        lines = mask[t].astype(F32)
        lines = rows_of([lines, lines])
        lines = lanes([lines] * LOCAL)
        for half in range(2):
            parts = []
            for p in range(2):
                mixed = dot(mix_x[pl.ds((2 * p + half) * 2 * N, 2 * N), :], data[t])
                mixed = mixed.reshape(32, 8, LOCAL * N) * lines[None]
                parts.append(mixed.reshape(2 * N, LOCAL * N).astype(BF16))
            stacked = rows_of(
                [lanes([parts[0][:, c * N : (c + 1) * N], parts[1][:, c * N : (c + 1) * N]]) for c in range(LOCAL)]
            )
            turned = dot(stacked, table[1])
            for h in range(2):
                for p in range(2):
                    for low in range(2):
                        piece = jnp.concatenate(
                            [
                                turned[c * 2 * N : (c + 1) * 2 * N, p * N : (p + 1) * N].reshape(16, 2, 8, N)[:, h]
                                for c in (low, 2 + low)
                            ],
                            axis=1,
                        )
                        send[t, pl.ds(half * 16, 16), h, :, pl.ds((2 * p + low) * N, N)] = piece.astype(BF16)

    def self_copy(t, h):
        return pltpu.make_async_copy(send.at[t, me, h], recv.at[t, me, h], self_sem.at[2 * t + h])

    def push_piece(n):
        t, h = n // 2, n % 2
        self_copy(t, h).start()

        def push(k, carry):
            to = lax.rem(me + k, SLABS)
            pltpu.make_async_remote_copy(
                src_ref=send.at[t, to, h], dst_ref=recv.at[t, me, h],
                send_sem=send_sem.at[n], recv_sem=recv_sem.at[n],
                device_id=(to, mg), device_id_type=MESH,
            ).start()
            return carry

        lax.fori_loop(1, SLABS, push, 0)

    def arrive(n):
        drain(recv.at[n // 2, pl.ds(0, SLABS - 1), n % 2], recv_sem.at[n])
        self_copy(n // 2, n % 2).wait()

    def drain(view, sem):
        pltpu.make_async_copy(view, view, sem).wait()

    def to_ring(source, target, ssem, rsem):
        for k in (2, 1, 3):
            to = lax.rem(place + k, RING)
            pltpu.make_async_remote_copy(
                src_ref=source(to), dst_ref=target, send_sem=ssem, recv_sem=rsem,
                device_id=(me, side * RING + to), device_id_type=MESH,
            ).start()

    def ring_start(part, land, sem):
        to_ring(lambda to: part.at[to], land.at[place], sem.at[0], sem.at[1])

    def ring_sum(part, land, half, sem, lead):
        drain(land.at[pl.ds(0, RING - 1)], sem.at[1])

        def one(i, carry):
            land[place, i] = part[place, i]
            value = land[0, i].astype(F32)
            for j in range(1, RING):
                value = value + land[j, i].astype(F32)
            half[0, i] = value.astype(BF16)
            return carry

        lax.fori_loop(0, lead, one, 0)
        pltpu.make_async_remote_copy(
            src_ref=half.at[0], dst_ref=half.at[1], send_sem=sem.at[2], recv_sem=sem.at[3],
            device_id=(me, (1 - side) * RING + place), device_id_type=MESH,
        ).start()

    def pair_sum(half, total, sem, lead):
        drain(half.at[1], sem.at[3])

        def one(i, carry):
            total[place, i] = (half[0, i].astype(F32) + half[1, i].astype(F32)).astype(BF16)
            return carry

        lax.fori_loop(0, lead, one, 0)
        to_ring(lambda to: total.at[place], total.at[place], sem.at[4], sem.at[5])

    def ring_end(total, sem):
        drain(total.at[pl.ds(0, RING - 1)], sem.at[5])

    def ring_spent(part, half, total, sem):
        drain(part.at[pl.ds(0, RING - 1)], sem.at[0])
        drain(half.at[0], sem.at[2])
        drain(total.at[pl.ds(0, RING - 1)], sem.at[4])

    data_chunk(0)
    pl.semaphore_wait(barrier, SLABS - 1 + GROUPS - 1)
    push_piece(0)
    push_piece(1)

    def push_mask(k, carry):
        to = lax.rem(me + k, SLABS)
        pltpu.make_async_remote_copy(
            src_ref=own_mask, dst_ref=all_mask.at[me],
            send_sem=mask_send, recv_sem=mask_recv,
            device_id=(to, mg), device_id_type=MESH,
        ).start()
        return carry

    lax.fori_loop(1, SLABS, push_mask, 0)

    data_chunk(1)
    push_piece(2)
    push_piece(3)

    def later_chunk(t, carry):
        data_chunk(t)
        return carry

    lax.fori_loop(2, PTS, later_chunk, 0)

    loads[5].wait()
    rows = basis[...].astype(F32).reshape(2 * PTS, 4 * PTS)
    _, col = iotas(2 * PTS, 4 * PTS)
    for l in range(2):
        mine = jnp.sum(jnp.where(col == 2 * mg + l, rows, 0.0), axis=1, keepdims=True)
        weight[l] = jnp.broadcast_to(mine, (2 * PTS, N))
    loads[2].wait()
    row, col = iotas(2 * N, 2 * N)
    untie = as_bf16(col == 2 * (row % N) + row // N)
    for x in range(LOCAL):
        pair = dot(untie, lanes([coef[0, x], coef[1, x]]))
        for t in range(PTS):
            re = im = None
            for l in range(2):
                b_re, b_im = weight[l, pl.ds(t, 1)], weight[l, pl.ds(PTS + t, 1)]
                x_re = pair[:N, l * N : (l + 1) * N]
                x_im = pair[N:, l * N : (l + 1) * N]
                r, i = b_re * x_re - b_im * x_im, b_re * x_im + b_im * x_re
                re, im = (r, i) if re is None else (re + r, im + i)
            image_part[:, t, 0, x] = re.astype(BF16).reshape(RING, QUARTER, N)
            image_part[:, t, 1, x] = im.astype(BF16).reshape(RING, QUARTER, N)
    ring_start(image_part, image_land, image_sem)

    loads[3].wait()
    for x in range(LOCAL):
        both = dot(untie, lanes([maps[c, x] for c in range(LOCAL)]))
        sens_re[x] = both[:N]
        sens_im[x] = both[N:]
    ring_sum(image_part, image_land, image_half, image_sem, PTS)
    loads[4].wait()
    for x in range(LOCAL):
        angle = (field[x] & (STEPS_CYCLE - 1)).astype(F32) * (2.0 * math.pi / STEPS_CYCLE)
        c1, s1 = jnp.cos(angle), jnp.sin(angle)
        c2, s2 = c1 * c1 - s1 * s1, 2.0 * (c1 * s1)
        c3, s3 = c2 * c1 - s2 * s1, s2 * c1 + c2 * s1
        c4, s4 = c2 * c2 - s2 * s2, 2.0 * (c2 * s2)
        for t, (c, s) in enumerate([(c1, s1), (c2, s2), (c3, s3), (c4, s4)]):
            cosine[t, x] = c
            sine[t, x] = s
    pair_sum(image_half, image_all, image_sem, PTS)
    row, col = iotas(2 * N, 8 * N)
    spread = as_bf16(
        (row // N == col // (4 * N)) & (row % N == 4 * ((col % (4 * N)) // 16) + col % 4)
    )
    wide = dot(table[0], spread)
    for j in range(4):
        mix_y[j] = jnp.where((col // 4) % 4 == j, wide, 0.0).astype(BF16)

    mask_view = all_mask.at[pl.ds(0, SLABS - 1)]
    pltpu.make_async_copy(mask_view, mask_view, mask_recv).wait()
    all_mask[me] = own_mask[...]
    row, col = iotas(N, SLABS * 16)
    everything = all_mask[...].reshape(SLABS * 16, N)
    for t in range(PTS):
        pick = as_bf16((col // 16 == row // 4) & (col % 4 == row % 4) & ((col // 4) % 4 == t))
        mask_full[t] = dot(pick, everything)

    def model_term(t):
        def one(x, carry):
            i_re = image_all[:, t, 0, x].reshape(N, N).astype(F32)
            i_im = image_all[:, t, 1, x].reshape(N, N).astype(F32)
            c, s = cosine[t, x], sine[t, x]
            t_re, t_im = c * i_re - s * i_im, s * i_re + c * i_im
            s_re, s_im = sens_re[x], sens_im[x]
            stack = []
            for k in range(LOCAL):
                a, b = s_re[:, k * N : (k + 1) * N], s_im[:, k * N : (k + 1) * N]
                stack.append(lanes([(a * t_re - b * t_im).astype(BF16), (a * t_im + b * t_re).astype(BF16)]))
            depth = dot(rows_of(stack), table[0]).astype(BF16)
            planes = rows_of(
                [lanes([depth[k * N : (k + 1) * N, p * N : (p + 1) * N] for k in range(LOCAL)]) for p in range(2)]
            )
            lines = dot(table[1], planes)
            m = lanes([mask_full[t]] * LOCAL)
            lines = rows_of([(lines[:N] * m).astype(BF16), (lines[N:] * m).astype(BF16)])
            back = dot(table[0], lines).astype(BF16)
            stack = rows_of(
                [lanes([back[p * N : (p + 1) * N, k * N : (k + 1) * N] for p in range(2)]) for k in range(LOCAL)]
            )
            back = dot(stack, table[1])
            q_re = q_im = None
            for k in range(LOCAL):
                a, b = s_re[:, k * N : (k + 1) * N], s_im[:, k * N : (k + 1) * N]
                r, i = back[k * N : (k + 1) * N, :N], back[k * N : (k + 1) * N, N:]
                u, v = a * r + b * i, a * i - b * r
                q_re, q_im = (u, v) if q_re is None else (q_re + u, q_im + v)
            model[t, x, 0] = q_re
            model[t, x, 1] = q_im
            return carry

        lax.fori_loop(0, LOCAL, one, 0)

    def model_step(t, carry):
        model_term(t)
        return carry

    ring_end(image_all, image_sem)
    arrive(0)
    push_piece(4)
    lax.fori_loop(0, 2, model_step, 0)
    arrive(1)
    push_piece(5)
    lax.fori_loop(2, PTS, model_step, 0)

    def data_term(n):
        t, h = n // 2, n % 2

        def one(j, carry):
            x = 2 * h + j
            arrived = recv[t, :, h].reshape(SLABS * 16, 4 * N)
            q_re, q_im = model[t, x, 0], model[t, x, 1]
            for high in range(2):
                mix = mix_y[2 * high + j]
                plane = dot(mix[:, : 4 * N], arrived[:, : 2 * N]) + dot(mix[:, 4 * N :], arrived[:, 2 * N :])
                s_re = sens_re[x, :, pl.ds(high * 2 * N, 2 * N)]
                s_im = sens_im[x, :, pl.ds(high * 2 * N, 2 * N)]
                r, i = plane[:N], plane[N:]
                u, v = s_re * r + s_im * i, s_re * i - s_im * r
                q_re = q_re - u[:, :N] - u[:, N:]
                q_im = q_im - v[:, :N] - v[:, N:]
            comb_part[n, :, 0, j] = q_re.astype(BF16).reshape(RING, QUARTER, N)
            comb_part[n, :, 1, j] = q_im.astype(BF16).reshape(RING, QUARTER, N)
            return carry

        lax.fori_loop(0, 2, one, 0)
    def middle(n):
        ring_sum(comb_part.at[n], comb_land.at[n], comb_half.at[n], comb_sem.at[n], 2)

    def last(n):
        pair_sum(comb_half.at[n], comb_all.at[n], comb_sem.at[n], 2)

    def accumulate(n, final):
        t, h = n // 2, n % 2
        if not (final and n == PIECES - 1):
            ring_end(comb_all.at[n], comb_sem.at[n])
        for j in range(2):
            x = 2 * h + j
            q_re = comb_all[n, :, 0, j].reshape(N, N).astype(F32)
            q_im = comb_all[n, :, 1, j].reshape(N, N).astype(F32)
            c, s = cosine[t, x], sine[t, x]
            w_re, w_im = c * q_re + s * q_im, c * q_im - s * q_re
            for l in range(2):
                b_re, b_im = weight[l, pl.ds(t, 1)], weight[l, pl.ds(PTS + t, 1)]
                g_re = grad[l, x, 0] + (b_re * w_re + b_im * w_im)
                g_im = grad[l, x, 1] + (b_re * w_im - b_im * w_re)
                if final:
                    out_ref[l, x, pl.ds(0, N, stride=2), :] = g_re
                    out_ref[l, x, pl.ds(1, N, stride=2), :] = g_im
                else:
                    grad[l, x, 0] = g_re
                    grad[l, x, 1] = g_im

    grad[...] = jnp.zeros(grad.shape, F32)

    def begin(n):
        data_term(n)
        ring_start(comb_part.at[n], comb_land.at[n], comb_sem.at[n])

    begin(0)
    begin(1)
    arrive(2)
    begin(2)
    arrive(3)
    begin(3)
    push_piece(6)
    arrive(4)
    begin(4)
    for n in range(4):
        middle(n)
    arrive(5)
    begin(5)
    for n in range(4):
        last(n)
    middle(4)
    push_piece(7)
    arrive(6)
    begin(6)
    for n in range(4):
        accumulate(n, False)
    last(4)
    middle(5)
    arrive(7)
    data_term(PIECES - 1)
    end_part, end_all = comb_part.at[PIECES - 1], comb_all.at[PIECES - 1]

    def slot(ref, q, half):
        return ref.at[q, :, :, pl.ds(pl.multiple_of(half * ROWS, ROWS), ROWS)]

    def to_group(source, target, ssem, rsem):
        for across, k in ((1, 2), (1, 1), (1, 3), (0, 2), (1, 0), (0, 1), (0, 3)):
            to_side = lax.rem(side + across, 2)
            to = lax.rem(place + k, RING)
            pltpu.make_async_remote_copy(
                src_ref=source(to, to_side), dst_ref=target, send_sem=ssem, recv_sem=rsem,
                device_id=(me, to_side * RING + to), device_id_type=MESH,
            ).start()

    to_group(lambda q, half: slot(end_part, q, half), end_land.at[mg], end_sem.at[0], end_sem.at[1])
    middle(6)
    last(5)
    drain(end_land.at[pl.ds(0, GROUPS - 1)], end_sem.at[1])
    end_land[mg] = slot(end_part, place, side)[...]
    value = end_land[0].astype(F32)
    for j in range(1, GROUPS):
        value = value + end_land[j].astype(F32)
    slot(end_all, place, side)[...] = value.astype(BF16)
    mine = slot(end_all, place, side)
    to_group(lambda q, half: mine, mine, end_sem.at[2], end_sem.at[3])
    last(6)
    accumulate(4, False)
    accumulate(5, False)
    accumulate(6, True)
    drain(end_land.at[pl.ds(0, GROUPS - 1)], end_sem.at[3])
    accumulate(PIECES - 1, True)

    def spent(n, carry):
        drain(send.at[n // 2, pl.ds(0, SLABS - 1), lax.rem(n, 2)], send_sem.at[n])

        @pl.when(n < PIECES - 1)
        def _():
            ring_spent(comb_part.at[n], comb_half.at[n], comb_all.at[n], comb_sem.at[n])

        return carry

    lax.fori_loop(0, PIECES, spent, 0)
    ring_spent(image_part, image_half, image_all, image_sem)
    drain(end_land.at[pl.ds(0, GROUPS - 1)], end_sem.at[0])
    drain(end_land.at[pl.ds(0, GROUPS - 1)], end_sem.at[2])
    pltpu.make_async_copy(mask_view, mask_view, mask_send).wait()


def step(coef, basis, maps, field, data, mask):
    any_space = pl.BlockSpec(memory_space=pl.ANY)
    dma = pltpu.SemaphoreType.DMA
    image = (PTS, 2, LOCAL, QUARTER, N)
    comb = (2, 2, QUARTER, N)
    scratch = [
        pltpu.VMEM((2, LOCAL, 2 * N, N), BF16),
        pltpu.VMEM((2, PTS, 4 * PTS), BF16),
        pltpu.VMEM((LOCAL, LOCAL, 2 * N, N), BF16),
        pltpu.VMEM((LOCAL, N, N), I32),
        pltpu.VMEM((PTS, 4, N), I32),
        pltpu.VMEM((2, 2 * N, 2 * N), BF16),
        pltpu.VMEM((PTS, 8 * N, LOCAL * N), BF16),
        pltpu.VMEM((8 * N, 8 * N), BF16),
        pltpu.VMEM((4, 2 * N, 8 * N), BF16),
        pltpu.VMEM((PTS, SLABS, 2, 16, 4 * N), BF16),
        pltpu.VMEM((PTS, SLABS, 2, 16, 4 * N), BF16),
        pltpu.VMEM((16, N), BF16),
        pltpu.VMEM((SLABS, 16, N), BF16),
        pltpu.VMEM((PTS, N, N), F32),
        pltpu.VMEM((LOCAL, N, LOCAL * N), F32),
        pltpu.VMEM((LOCAL, N, LOCAL * N), F32),
        pltpu.VMEM((PTS, LOCAL, N, N), F32),
        pltpu.VMEM((PTS, LOCAL, N, N), F32),
        pltpu.VMEM((2, 2 * PTS, N), F32),
        pltpu.VMEM((PTS, LOCAL, 2, N, N), F32),
        pltpu.VMEM((2, LOCAL, 2, N, N), F32),
        pltpu.VMEM((RING,) + image, BF16),
        pltpu.VMEM((RING,) + image, BF16),
        pltpu.VMEM((2,) + image, BF16),
        pltpu.VMEM((RING,) + image, BF16),
        pltpu.VMEM((PIECES, RING) + comb, BF16),
        pltpu.VMEM((PIECES, RING) + comb, BF16),
        pltpu.VMEM((PIECES, 2) + comb, BF16),
        pltpu.VMEM((PIECES, RING) + comb, BF16),
        pltpu.VMEM((GROUPS, 2, 2, ROWS, N), BF16),
        dma((6,)), dma((PTS, LOCAL)), dma((PIECES,)), dma((PIECES,)), dma((PIECES,)), dma, dma,
        dma((6,)), dma((PIECES, 6)), dma((4,)),
    ]
    out = pl.pallas_call(
        body,
        out_shape=jax.ShapeDtypeStruct((2, LOCAL, 2 * N, N), F32),
        in_specs=[any_space] * 7,
        out_specs=pl.BlockSpec(memory_space=pltpu.VMEM),
        scratch_shapes=scratch,
        compiler_params=pltpu.CompilerParams(
            collective_id=0, has_side_effects=True, vmem_limit_bytes=44 << 20
        ),
    )(
        *[
            pltpu.with_memory_space_constraint(value, pltpu.HBM)
            for value in (
                coef.reshape(2, LOCAL, 2 * N, N),
                jnp.transpose(basis, (0, 2, 1)),
                maps.reshape(LOCAL, LOCAL, 2 * N, N),
                field,
                data.reshape(LOCAL, PTS, 8 * N, N),
                mask,
                jnp.asarray(dft_pair()),
            )
        ]
    )
    return out.reshape(2, LOCAL, N, 2, N)


def solution(mesh):
    in_specs = (
        P("coil", "space", None, None, None),
        P(),
        P("coil", "space", None, None, None),
        P("space", None, None),
        P("coil", None, None, "space", None, None),
        P(None, "space", None),
    )
    out_specs = P("coil", "space", None, None, None)
    return jax.shard_map(step, mesh=mesh, in_specs=in_specs, out_specs=out_specs, check_vma=False)
```

```python
import math

import jax
import jax.numpy as jnp
import numpy as np
from jax import lax
from jax.experimental import pallas as pl
from jax.experimental.pallas import tpu as pltpu
from jax.sharding import PartitionSpec as P

STEPS_CYCLE = 256
N = 128
PTS = 4
LOCAL = 4
SLABS = 32
GROUPS = 8
RING = 4
QUARTER = N // RING
ROWS = N // GROUPS
PIECES = 2 * PTS
F32 = jnp.float32
BF16 = jnp.bfloat16
I32 = jnp.int32
MESH = pl.DeviceIdType.MESH


def dft_pair():
    index = np.arange(N)
    angle = (index[:, None] * index[None, :] % N).astype(np.float32) * np.float32(2.0 * math.pi / N)
    cosine = np.cos(angle) / np.float32(math.sqrt(N))
    sine = np.sin(angle) / np.float32(math.sqrt(N))
    inverse = np.block([[cosine, -sine], [sine, cosine]])
    return np.stack([inverse, inverse.T]).astype(jnp.bfloat16)


def dot(a, b):
    return jnp.dot(a, b, preferred_element_type=F32)


def iotas(rows, cols):
    return (
        lax.broadcasted_iota(I32, (rows, cols), 0),
        lax.broadcasted_iota(I32, (rows, cols), 1),
    )


def as_bf16(condition):
    return jnp.where(condition, 1.0, 0.0).astype(BF16)


def lanes(parts):
    return jnp.concatenate(parts, axis=1)


def rows_of(parts):
    return jnp.concatenate(parts, axis=0)


def body(
    coef_hbm, basis_hbm, maps_hbm, field_hbm, data_hbm, mask_hbm, table_hbm, out_ref,
    coef, basis, maps, field, mask, table, data, mix_x, mix_y, send, recv, own_mask, all_mask, mask_full,
    sens_re, sens_im, cosine, sine, weight, model, grad,
    image_part, image_land, image_half, image_all, comb_part, comb_land, comb_half, comb_all, end_land,
    load_sem, data_sem, self_sem, send_sem, recv_sem, mask_send, mask_recv, image_sem, comb_sem, end_sem,
):
    me = lax.axis_index("space")
    mg = lax.axis_index("coil")
    side = mg // RING
    place = lax.rem(mg, RING)

    barrier = pltpu.get_barrier_semaphore()

    def greet_space(k, carry):
        pl.semaphore_signal(barrier, inc=1, device_id=(lax.rem(me + k, SLABS), mg), device_id_type=MESH)
        return carry

    def greet_coil(k, carry):
        pl.semaphore_signal(barrier, inc=1, device_id=(me, lax.rem(mg + k, GROUPS)), device_id_type=MESH)
        return carry

    lax.fori_loop(1, SLABS, greet_space, 0)
    lax.fori_loop(1, GROUPS, greet_coil, 0)

    loads = [
        pltpu.make_async_copy(src, dst, load_sem.at[i])
        for i, (src, dst) in enumerate(
            [
                (table_hbm, table), (mask_hbm, mask), (coef_hbm, coef),
                (maps_hbm, maps), (field_hbm, field), (basis_hbm, basis),
            ]
        )
    ]

    def data_load(t, c):
        return pltpu.make_async_copy(
            data_hbm.at[c, t], data.at[t, :, pl.ds(c * N, N)], data_sem.at[t, c]
        )

    loads[0].start()
    loads[1].start()
    for c in range(LOCAL):
        data_load(0, c).start()
    for load in loads[2:]:
        load.start()
    for t in range(1, PTS):
        for c in range(LOCAL):
            data_load(t, c).start()
    loads[0].wait()

    row, col = iotas(2 * N, 8 * N)
    spread = as_bf16((row % N == col // 8) & (row // N == col % 2))
    wide = dot(table[0], spread).astype(BF16)
    row, col = iotas(2 * N, N // 2)
    repeat = as_bf16(col == row // 4)
    row, col = iotas(2 * N, 8 * N)
    same_line = row % 4 == (col // 2) % 4
    for block in range(4):
        part = dot(repeat, wide[block * (N // 2) : (block + 1) * (N // 2)])
        mix_x[pl.ds(block * 2 * N, 2 * N), :] = jnp.where(same_line, part, 0.0).astype(BF16)
    loads[1].wait()
    for t in range(PTS):
        own_mask[pl.ds(t * 4, 4), :] = mask[t].astype(F32).astype(BF16)

    def data_chunk(t):
        for c in range(LOCAL):
            data_load(t, c).wait()
        lines = mask[t].astype(F32)
        lines = rows_of([lines, lines])
        lines = lanes([lines] * LOCAL)
        for half in range(2):
            parts = []
            for p in range(2):
                mixed = dot(mix_x[pl.ds((2 * p + half) * 2 * N, 2 * N), :], data[t])
                mixed = mixed.reshape(32, 8, LOCAL * N) * lines[None]
                parts.append(mixed.reshape(2 * N, LOCAL * N).astype(BF16))
            stacked = rows_of(
                [lanes([parts[0][:, c * N : (c + 1) * N], parts[1][:, c * N : (c + 1) * N]]) for c in range(LOCAL)]
            )
            turned = dot(stacked, table[1])
            for h in range(2):
                for p in range(2):
                    for low in range(2):
                        piece = jnp.concatenate(
                            [
                                turned[c * 2 * N : (c + 1) * 2 * N, p * N : (p + 1) * N].reshape(16, 2, 8, N)[:, h]
                                for c in (low, 2 + low)
                            ],
                            axis=1,
                        )
                        send[t, pl.ds(half * 16, 16), h, :, pl.ds((2 * p + low) * N, N)] = piece.astype(BF16)

    def self_copy(t, h):
        return pltpu.make_async_copy(send.at[t, me, h], recv.at[t, me, h], self_sem.at[2 * t + h])

    def push_piece(n):
        t, h = n // 2, n % 2
        self_copy(t, h).start()

        def push(k, carry):
            to = lax.rem(me + k, SLABS)
            pltpu.make_async_remote_copy(
                src_ref=send.at[t, to, h], dst_ref=recv.at[t, me, h],
                send_sem=send_sem.at[n], recv_sem=recv_sem.at[n],
                device_id=(to, mg), device_id_type=MESH,
            ).start()
            return carry

        lax.fori_loop(1, SLABS, push, 0)

    def arrive(n):
        drain(recv.at[n // 2, pl.ds(0, SLABS - 1), n % 2], recv_sem.at[n])
        self_copy(n // 2, n % 2).wait()

    def drain(view, sem):
        pltpu.make_async_copy(view, view, sem).wait()

    def to_ring(source, target, ssem, rsem):
        for k in (2, 1, 3):
            to = lax.rem(place + k, RING)
            pltpu.make_async_remote_copy(
                src_ref=source(to), dst_ref=target, send_sem=ssem, recv_sem=rsem,
                device_id=(me, side * RING + to), device_id_type=MESH,
            ).start()

    def ring_start(part, land, sem):
        to_ring(lambda to: part.at[to], land.at[place], sem.at[0], sem.at[1])

    def ring_sum(part, land, half, sem, lead):
        drain(land.at[pl.ds(0, RING - 1)], sem.at[1])

        def one(i, carry):
            land[place, i] = part[place, i]
            value = land[0, i].astype(F32)
            for j in range(1, RING):
                value = value + land[j, i].astype(F32)
            half[0, i] = value.astype(BF16)
            return carry

        lax.fori_loop(0, lead, one, 0)
        pltpu.make_async_remote_copy(
            src_ref=half.at[0], dst_ref=half.at[1], send_sem=sem.at[2], recv_sem=sem.at[3],
            device_id=(me, (1 - side) * RING + place), device_id_type=MESH,
        ).start()

    def pair_sum(half, total, sem, lead):
        drain(half.at[1], sem.at[3])

        def one(i, carry):
            total[place, i] = (half[0, i].astype(F32) + half[1, i].astype(F32)).astype(BF16)
            return carry

        lax.fori_loop(0, lead, one, 0)
        to_ring(lambda to: total.at[place], total.at[place], sem.at[4], sem.at[5])

    def ring_end(total, sem):
        drain(total.at[pl.ds(0, RING - 1)], sem.at[5])

    def ring_spent(part, half, total, sem):
        drain(part.at[pl.ds(0, RING - 1)], sem.at[0])
        drain(half.at[0], sem.at[2])
        drain(total.at[pl.ds(0, RING - 1)], sem.at[4])

    data_chunk(0)
    pl.semaphore_wait(barrier, SLABS - 1 + GROUPS - 1)
    push_piece(0)
    push_piece(1)

    def push_mask(k, carry):
        to = lax.rem(me + k, SLABS)
        pltpu.make_async_remote_copy(
            src_ref=own_mask, dst_ref=all_mask.at[me],
            send_sem=mask_send, recv_sem=mask_recv,
            device_id=(to, mg), device_id_type=MESH,
        ).start()
        return carry

    lax.fori_loop(1, SLABS, push_mask, 0)

    loads[5].wait()
    rows = basis[...].astype(F32).reshape(2 * PTS, 4 * PTS)
    _, col = iotas(2 * PTS, 4 * PTS)
    for l in range(2):
        mine = jnp.sum(jnp.where(col == 2 * mg + l, rows, 0.0), axis=1, keepdims=True)
        weight[l] = jnp.broadcast_to(mine, (2 * PTS, N))
    loads[2].wait()
    row, col = iotas(2 * N, 2 * N)
    untie = as_bf16(col == 2 * (row % N) + row // N)
    for x in range(LOCAL):
        pair = dot(untie, lanes([coef[0, x], coef[1, x]]))
        for t in range(PTS):
            re = im = None
            for l in range(2):
                b_re, b_im = weight[l, pl.ds(t, 1)], weight[l, pl.ds(PTS + t, 1)]
                x_re = pair[:N, l * N : (l + 1) * N]
                x_im = pair[N:, l * N : (l + 1) * N]
                r, i = b_re * x_re - b_im * x_im, b_re * x_im + b_im * x_re
                re, im = (r, i) if re is None else (re + r, im + i)
            image_part[:, t, 0, x] = re.astype(BF16).reshape(RING, QUARTER, N)
            image_part[:, t, 1, x] = im.astype(BF16).reshape(RING, QUARTER, N)
    ring_start(image_part, image_land, image_sem)

    data_chunk(1)
    push_piece(2)

    def later_chunk(t, carry):
        data_chunk(t)
        return carry

    lax.fori_loop(2, PTS, later_chunk, 0)

    loads[3].wait()
    for x in range(LOCAL):
        both = dot(untie, lanes([maps[c, x] for c in range(LOCAL)]))
        sens_re[x] = both[:N]
        sens_im[x] = both[N:]
    ring_sum(image_part, image_land, image_half, image_sem, PTS)
    push_piece(3)
    loads[4].wait()
    for x in range(LOCAL):
        angle = (field[x] & (STEPS_CYCLE - 1)).astype(F32) * (2.0 * math.pi / STEPS_CYCLE)
        c1, s1 = jnp.cos(angle), jnp.sin(angle)
        c2, s2 = c1 * c1 - s1 * s1, 2.0 * (c1 * s1)
        c3, s3 = c2 * c1 - s2 * s1, s2 * c1 + c2 * s1
        c4, s4 = c2 * c2 - s2 * s2, 2.0 * (c2 * s2)
        for t, (c, s) in enumerate([(c1, s1), (c2, s2), (c3, s3), (c4, s4)]):
            cosine[t, x] = c
            sine[t, x] = s
    pair_sum(image_half, image_all, image_sem, PTS)
    arrive(0)
    push_piece(4)
    row, col = iotas(2 * N, 8 * N)
    spread = as_bf16(
        (row // N == col // (4 * N)) & (row % N == 4 * ((col % (4 * N)) // 16) + col % 4)
    )
    wide = dot(table[0], spread)
    for j in range(4):
        mix_y[j] = jnp.where((col // 4) % 4 == j, wide, 0.0).astype(BF16)

    mask_view = all_mask.at[pl.ds(0, SLABS - 1)]
    pltpu.make_async_copy(mask_view, mask_view, mask_recv).wait()
    all_mask[me] = own_mask[...]
    row, col = iotas(N, SLABS * 16)
    everything = all_mask[...].reshape(SLABS * 16, N)
    for t in range(PTS):
        pick = as_bf16((col // 16 == row // 4) & (col % 4 == row % 4) & ((col // 4) % 4 == t))
        mask_full[t] = dot(pick, everything)

    def model_term(t):
        def one(x, carry):
            i_re = image_all[:, t, 0, x].reshape(N, N).astype(F32)
            i_im = image_all[:, t, 1, x].reshape(N, N).astype(F32)
            c, s = cosine[t, x], sine[t, x]
            t_re, t_im = c * i_re - s * i_im, s * i_re + c * i_im
            s_re, s_im = sens_re[x], sens_im[x]
            stack = []
            for k in range(LOCAL):
                a, b = s_re[:, k * N : (k + 1) * N], s_im[:, k * N : (k + 1) * N]
                stack.append(lanes([(a * t_re - b * t_im).astype(BF16), (a * t_im + b * t_re).astype(BF16)]))
            depth = dot(rows_of(stack), table[0]).astype(BF16)
            planes = rows_of(
                [lanes([depth[k * N : (k + 1) * N, p * N : (p + 1) * N] for k in range(LOCAL)]) for p in range(2)]
            )
            lines = dot(table[1], planes)
            m = lanes([mask_full[t]] * LOCAL)
            lines = rows_of([(lines[:N] * m).astype(BF16), (lines[N:] * m).astype(BF16)])
            back = dot(table[0], lines).astype(BF16)
            stack = rows_of(
                [lanes([back[p * N : (p + 1) * N, k * N : (k + 1) * N] for p in range(2)]) for k in range(LOCAL)]
            )
            back = dot(stack, table[1])
            q_re = q_im = None
            for k in range(LOCAL):
                a, b = s_re[:, k * N : (k + 1) * N], s_im[:, k * N : (k + 1) * N]
                r, i = back[k * N : (k + 1) * N, :N], back[k * N : (k + 1) * N, N:]
                u, v = a * r + b * i, a * i - b * r
                q_re, q_im = (u, v) if q_re is None else (q_re + u, q_im + v)
            model[t, x, 0] = q_re
            model[t, x, 1] = q_im
            return carry

        lax.fori_loop(0, LOCAL, one, 0)

    def model_step(t, carry):
        model_term(t)
        return carry

    ring_end(image_all, image_sem)
    arrive(1)
    push_piece(5)
    lax.fori_loop(0, PTS, model_step, 0)

    def data_term(n):
        t, h = n // 2, n % 2

        def one(j, carry):
            x = 2 * h + j
            arrived = recv[t, :, h].reshape(SLABS * 16, 4 * N)
            q_re, q_im = model[t, x, 0], model[t, x, 1]
            for high in range(2):
                mix = mix_y[2 * high + j]
                plane = dot(mix[:, : 4 * N], arrived[:, : 2 * N]) + dot(mix[:, 4 * N :], arrived[:, 2 * N :])
                s_re = sens_re[x, :, pl.ds(high * 2 * N, 2 * N)]
                s_im = sens_im[x, :, pl.ds(high * 2 * N, 2 * N)]
                r, i = plane[:N], plane[N:]
                u, v = s_re * r + s_im * i, s_re * i - s_im * r
                q_re = q_re - u[:, :N] - u[:, N:]
                q_im = q_im - v[:, :N] - v[:, N:]
            comb_part[n, :, 0, j] = q_re.astype(BF16).reshape(RING, QUARTER, N)
            comb_part[n, :, 1, j] = q_im.astype(BF16).reshape(RING, QUARTER, N)
            return carry

        lax.fori_loop(0, 2, one, 0)
    def middle(n):
        ring_sum(comb_part.at[n], comb_land.at[n], comb_half.at[n], comb_sem.at[n], 2)

    def last(n):
        pair_sum(comb_half.at[n], comb_all.at[n], comb_sem.at[n], 2)

    def accumulate(n, final):
        t, h = n // 2, n % 2
        if not (final and n == PIECES - 1):
            ring_end(comb_all.at[n], comb_sem.at[n])
        for j in range(2):
            x = 2 * h + j
            q_re = comb_all[n, :, 0, j].reshape(N, N).astype(F32)
            q_im = comb_all[n, :, 1, j].reshape(N, N).astype(F32)
            c, s = cosine[t, x], sine[t, x]
            w_re, w_im = c * q_re + s * q_im, c * q_im - s * q_re
            for l in range(2):
                b_re, b_im = weight[l, pl.ds(t, 1)], weight[l, pl.ds(PTS + t, 1)]
                g_re = grad[l, x, 0] + (b_re * w_re + b_im * w_im)
                g_im = grad[l, x, 1] + (b_re * w_im - b_im * w_re)
                if final:
                    out_ref[l, x, pl.ds(0, N, stride=2), :] = g_re
                    out_ref[l, x, pl.ds(1, N, stride=2), :] = g_im
                else:
                    grad[l, x, 0] = g_re
                    grad[l, x, 1] = g_im

    grad[...] = jnp.zeros(grad.shape, F32)

    def begin(n):
        data_term(n)
        ring_start(comb_part.at[n], comb_land.at[n], comb_sem.at[n])

    begin(0)
    begin(1)
    arrive(2)
    begin(2)
    arrive(3)
    begin(3)
    push_piece(6)
    arrive(4)
    begin(4)
    for n in range(4):
        middle(n)
    arrive(5)
    begin(5)
    for n in range(4):
        last(n)
    middle(4)
    push_piece(7)
    arrive(6)
    begin(6)
    for n in range(4):
        accumulate(n, False)
    last(4)
    middle(5)
    arrive(7)
    data_term(PIECES - 1)
    end_part, end_all = comb_part.at[PIECES - 1], comb_all.at[PIECES - 1]

    def slot(ref, q, half):
        return ref.at[q, :, :, pl.ds(pl.multiple_of(half * ROWS, ROWS), ROWS)]

    def to_group(source, target, ssem, rsem):
        for across, k in ((1, 2), (1, 1), (1, 3), (0, 2), (1, 0), (0, 1), (0, 3)):
            to_side = lax.rem(side + across, 2)
            to = lax.rem(place + k, RING)
            pltpu.make_async_remote_copy(
                src_ref=source(to, to_side), dst_ref=target, send_sem=ssem, recv_sem=rsem,
                device_id=(me, to_side * RING + to), device_id_type=MESH,
            ).start()

    to_group(lambda q, half: slot(end_part, q, half), end_land.at[mg], end_sem.at[0], end_sem.at[1])
    middle(6)
    last(5)
    drain(end_land.at[pl.ds(0, GROUPS - 1)], end_sem.at[1])
    end_land[mg] = slot(end_part, place, side)[...]
    value = end_land[0].astype(F32)
    for j in range(1, GROUPS):
        value = value + end_land[j].astype(F32)
    slot(end_all, place, side)[...] = value.astype(BF16)
    mine = slot(end_all, place, side)
    to_group(lambda q, half: mine, mine, end_sem.at[2], end_sem.at[3])
    last(6)
    accumulate(4, False)
    accumulate(5, False)
    accumulate(6, True)
    drain(end_land.at[pl.ds(0, GROUPS - 1)], end_sem.at[3])
    accumulate(PIECES - 1, True)

    def spent(n, carry):
        drain(send.at[n // 2, pl.ds(0, SLABS - 1), lax.rem(n, 2)], send_sem.at[n])

        @pl.when(n < PIECES - 1)
        def _():
            ring_spent(comb_part.at[n], comb_half.at[n], comb_all.at[n], comb_sem.at[n])

        return carry

    lax.fori_loop(0, PIECES, spent, 0)
    ring_spent(image_part, image_half, image_all, image_sem)
    drain(end_land.at[pl.ds(0, GROUPS - 1)], end_sem.at[0])
    drain(end_land.at[pl.ds(0, GROUPS - 1)], end_sem.at[2])
    pltpu.make_async_copy(mask_view, mask_view, mask_send).wait()


def step(coef, basis, maps, field, data, mask):
    any_space = pl.BlockSpec(memory_space=pl.ANY)
    dma = pltpu.SemaphoreType.DMA
    image = (PTS, 2, LOCAL, QUARTER, N)
    comb = (2, 2, QUARTER, N)
    scratch = [
        pltpu.VMEM((2, LOCAL, 2 * N, N), BF16),
        pltpu.VMEM((2, PTS, 4 * PTS), BF16),
        pltpu.VMEM((LOCAL, LOCAL, 2 * N, N), BF16),
        pltpu.VMEM((LOCAL, N, N), I32),
        pltpu.VMEM((PTS, 4, N), I32),
        pltpu.VMEM((2, 2 * N, 2 * N), BF16),
        pltpu.VMEM((PTS, 8 * N, LOCAL * N), BF16),
        pltpu.VMEM((8 * N, 8 * N), BF16),
        pltpu.VMEM((4, 2 * N, 8 * N), BF16),
        pltpu.VMEM((PTS, SLABS, 2, 16, 4 * N), BF16),
        pltpu.VMEM((PTS, SLABS, 2, 16, 4 * N), BF16),
        pltpu.VMEM((16, N), BF16),
        pltpu.VMEM((SLABS, 16, N), BF16),
        pltpu.VMEM((PTS, N, N), F32),
        pltpu.VMEM((LOCAL, N, LOCAL * N), F32),
        pltpu.VMEM((LOCAL, N, LOCAL * N), F32),
        pltpu.VMEM((PTS, LOCAL, N, N), F32),
        pltpu.VMEM((PTS, LOCAL, N, N), F32),
        pltpu.VMEM((2, 2 * PTS, N), F32),
        pltpu.VMEM((PTS, LOCAL, 2, N, N), F32),
        pltpu.VMEM((2, LOCAL, 2, N, N), F32),
        pltpu.VMEM((RING,) + image, BF16),
        pltpu.VMEM((RING,) + image, BF16),
        pltpu.VMEM((2,) + image, BF16),
        pltpu.VMEM((RING,) + image, BF16),
        pltpu.VMEM((PIECES, RING) + comb, BF16),
        pltpu.VMEM((PIECES, RING) + comb, BF16),
        pltpu.VMEM((PIECES, 2) + comb, BF16),
        pltpu.VMEM((PIECES, RING) + comb, BF16),
        pltpu.VMEM((GROUPS, 2, 2, ROWS, N), BF16),
        dma((6,)), dma((PTS, LOCAL)), dma((PIECES,)), dma((PIECES,)), dma((PIECES,)), dma, dma,
        dma((6,)), dma((PIECES, 6)), dma((4,)),
    ]
    out = pl.pallas_call(
        body,
        out_shape=jax.ShapeDtypeStruct((2, LOCAL, 2 * N, N), F32),
        in_specs=[any_space] * 7,
        out_specs=pl.BlockSpec(memory_space=pltpu.VMEM),
        scratch_shapes=scratch,
        compiler_params=pltpu.CompilerParams(
            collective_id=0, has_side_effects=True, vmem_limit_bytes=44 << 20
        ),
    )(
        *[
            pltpu.with_memory_space_constraint(value, pltpu.HBM)
            for value in (
                coef.reshape(2, LOCAL, 2 * N, N),
                jnp.transpose(basis, (0, 2, 1)),
                maps.reshape(LOCAL, LOCAL, 2 * N, N),
                field,
                data.reshape(LOCAL, PTS, 8 * N, N),
                mask,
                jnp.asarray(dft_pair()),
            )
        ]
    )
    return out.reshape(2, LOCAL, N, 2, N)


def solution(mesh):
    in_specs = (
        P("coil", "space", None, None, None),
        P(),
        P("coil", "space", None, None, None),
        P("space", None, None),
        P("coil", None, None, "space", None, None),
        P(None, "space", None),
    )
    out_specs = P("coil", "space", None, None, None)
    return jax.shard_map(step, mesh=mesh, in_specs=in_specs, out_specs=out_specs, check_vma=False)
```

```python
import math

import jax
import jax.numpy as jnp
import numpy as np
from jax import lax
from jax.experimental import pallas as pl
from jax.experimental.pallas import tpu as pltpu
from jax.sharding import PartitionSpec as P

STEPS_CYCLE = 256
N = 128
PTS = 4
LOCAL = 4
SLABS = 32
GROUPS = 8
RING = 4
QUARTER = N // RING
ROWS = N // GROUPS
PIECES = 2 * PTS
F32 = jnp.float32
BF16 = jnp.bfloat16
I32 = jnp.int32
MESH = pl.DeviceIdType.MESH


def dft_pair():
    index = np.arange(N)
    angle = (index[:, None] * index[None, :] % N).astype(np.float32) * np.float32(2.0 * math.pi / N)
    cosine = np.cos(angle) / np.float32(math.sqrt(N))
    sine = np.sin(angle) / np.float32(math.sqrt(N))
    inverse = np.block([[cosine, -sine], [sine, cosine]])
    return np.stack([inverse, inverse.T]).astype(jnp.bfloat16)


def dot(a, b):
    return jnp.dot(a, b, preferred_element_type=F32)


def iotas(rows, cols):
    return (
        lax.broadcasted_iota(I32, (rows, cols), 0),
        lax.broadcasted_iota(I32, (rows, cols), 1),
    )


def as_bf16(condition):
    return jnp.where(condition, 1.0, 0.0).astype(BF16)


def lanes(parts):
    return jnp.concatenate(parts, axis=1)


def rows_of(parts):
    return jnp.concatenate(parts, axis=0)


def body(
    coef_hbm, basis_hbm, maps_hbm, field_hbm, data_hbm, mask_hbm, table_hbm, out_ref,
    coef, basis, maps, field, mask, table, data, mix_x, mix_y, send, recv, own_mask, all_mask, mask_full,
    sens_re, sens_im, cosine, sine, weight, model, grad,
    image_part, image_land, image_half, image_all, comb_part, comb_land, comb_half, comb_all, end_land,
    load_sem, data_sem, self_sem, send_sem, recv_sem, mask_send, mask_recv, image_sem, comb_sem, end_sem,
):
    me = lax.axis_index("space")
    mg = lax.axis_index("coil")
    side = mg // RING
    place = lax.rem(mg, RING)

    barrier = pltpu.get_barrier_semaphore()

    def greet_space(k, carry):
        pl.semaphore_signal(barrier, inc=1, device_id=(lax.rem(me + k, SLABS), mg), device_id_type=MESH)
        return carry

    def greet_coil(k, carry):
        pl.semaphore_signal(barrier, inc=1, device_id=(me, lax.rem(mg + k, GROUPS)), device_id_type=MESH)
        return carry

    lax.fori_loop(1, SLABS, greet_space, 0)
    lax.fori_loop(1, GROUPS, greet_coil, 0)

    loads = [
        pltpu.make_async_copy(src, dst, load_sem.at[i])
        for i, (src, dst) in enumerate(
            [
                (table_hbm, table), (mask_hbm, mask), (coef_hbm, coef),
                (maps_hbm, maps), (field_hbm, field), (basis_hbm, basis),
            ]
        )
    ]

    def data_load(t, c):
        return pltpu.make_async_copy(
            data_hbm.at[c, t], data.at[t, :, pl.ds(c * N, N)], data_sem.at[t, c]
        )

    loads[0].start()
    loads[1].start()
    for c in range(LOCAL):
        data_load(0, c).start()
    for load in loads[2:]:
        load.start()
    for t in range(1, PTS):
        for c in range(LOCAL):
            data_load(t, c).start()
    loads[0].wait()

    row, col = iotas(2 * N, 8 * N)
    spread = as_bf16((row % N == col // 8) & (row // N == col % 2))
    wide = dot(table[0], spread).astype(BF16)
    row, col = iotas(2 * N, N // 2)
    repeat = as_bf16(col == row // 4)
    row, col = iotas(2 * N, 8 * N)
    same_line = row % 4 == (col // 2) % 4
    for block in range(4):
        part = dot(repeat, wide[block * (N // 2) : (block + 1) * (N // 2)])
        mix_x[pl.ds(block * 2 * N, 2 * N), :] = jnp.where(same_line, part, 0.0).astype(BF16)
    loads[1].wait()
    for t in range(PTS):
        own_mask[pl.ds(t * 4, 4), :] = mask[t].astype(F32).astype(BF16)

    def data_chunk(t):
        for c in range(LOCAL):
            data_load(t, c).wait()
        lines = mask[t].astype(F32)
        lines = rows_of([lines, lines])
        lines = lanes([lines] * LOCAL)
        for half in range(2):
            parts = []
            for p in range(2):
                mixed = dot(mix_x[pl.ds((2 * p + half) * 2 * N, 2 * N), :], data[t])
                mixed = mixed.reshape(32, 8, LOCAL * N) * lines[None]
                parts.append(mixed.reshape(2 * N, LOCAL * N).astype(BF16))
            stacked = rows_of(
                [lanes([parts[0][:, c * N : (c + 1) * N], parts[1][:, c * N : (c + 1) * N]]) for c in range(LOCAL)]
            )
            turned = dot(stacked, table[1])
            for h in range(2):
                for p in range(2):
                    for low in range(2):
                        piece = jnp.concatenate(
                            [
                                turned[c * 2 * N : (c + 1) * 2 * N, p * N : (p + 1) * N].reshape(16, 2, 8, N)[:, h]
                                for c in (low, 2 + low)
                            ],
                            axis=1,
                        )
                        send[t, pl.ds(half * 16, 16), h, :, pl.ds((2 * p + low) * N, N)] = piece.astype(BF16)

    def self_copy(t, h):
        return pltpu.make_async_copy(send.at[t, me, h], recv.at[t, me, h], self_sem.at[2 * t + h])

    def push_piece(n):
        t, h = n // 2, n % 2
        self_copy(t, h).start()

        def push(k, carry):
            to = lax.rem(me + k, SLABS)
            pltpu.make_async_remote_copy(
                src_ref=send.at[t, to, h], dst_ref=recv.at[t, me, h],
                send_sem=send_sem.at[n], recv_sem=recv_sem.at[n],
                device_id=(to, mg), device_id_type=MESH,
            ).start()
            return carry

        lax.fori_loop(1, SLABS, push, 0)

    def arrive(n):
        drain(recv.at[n // 2, pl.ds(0, SLABS - 1), n % 2], recv_sem.at[n])
        self_copy(n // 2, n % 2).wait()

    def drain(view, sem):
        pltpu.make_async_copy(view, view, sem).wait()

    def to_ring(source, target, ssem, rsem):
        for k in (2, 1, 3):
            to = lax.rem(place + k, RING)
            pltpu.make_async_remote_copy(
                src_ref=source(to), dst_ref=target, send_sem=ssem, recv_sem=rsem,
                device_id=(me, side * RING + to), device_id_type=MESH,
            ).start()

    def ring_start(part, land, sem):
        to_ring(lambda to: part.at[to], land.at[place], sem.at[0], sem.at[1])

    def ring_sum(part, land, half, sem, lead):
        drain(land.at[pl.ds(0, RING - 1)], sem.at[1])

        def one(i, carry):
            land[place, i] = part[place, i]
            value = land[0, i].astype(F32)
            for j in range(1, RING):
                value = value + land[j, i].astype(F32)
            half[0, i] = value.astype(BF16)
            return carry

        lax.fori_loop(0, lead, one, 0)
        pltpu.make_async_remote_copy(
            src_ref=half.at[0], dst_ref=half.at[1], send_sem=sem.at[2], recv_sem=sem.at[3],
            device_id=(me, (1 - side) * RING + place), device_id_type=MESH,
        ).start()

    def pair_sum(half, total, sem, lead):
        drain(half.at[1], sem.at[3])

        def one(i, carry):
            total[place, i] = (half[0, i].astype(F32) + half[1, i].astype(F32)).astype(BF16)
            return carry

        lax.fori_loop(0, lead, one, 0)
        to_ring(lambda to: total.at[place], total.at[place], sem.at[4], sem.at[5])

    def ring_end(total, sem):
        drain(total.at[pl.ds(0, RING - 1)], sem.at[5])

    def ring_spent(part, half, total, sem):
        drain(part.at[pl.ds(0, RING - 1)], sem.at[0])
        drain(half.at[0], sem.at[2])
        drain(total.at[pl.ds(0, RING - 1)], sem.at[4])

    data_chunk(0)
    pl.semaphore_wait(barrier, SLABS - 1 + GROUPS - 1)
    push_piece(0)
    push_piece(1)

    def push_mask(k, carry):
        to = lax.rem(me + k, SLABS)
        pltpu.make_async_remote_copy(
            src_ref=own_mask, dst_ref=all_mask.at[me],
            send_sem=mask_send, recv_sem=mask_recv,
            device_id=(to, mg), device_id_type=MESH,
        ).start()
        return carry

    lax.fori_loop(1, SLABS, push_mask, 0)

    loads[5].wait()
    rows = basis[...].astype(F32).reshape(2 * PTS, 4 * PTS)
    _, col = iotas(2 * PTS, 4 * PTS)
    for l in range(2):
        mine = jnp.sum(jnp.where(col == 2 * mg + l, rows, 0.0), axis=1, keepdims=True)
        weight[l] = jnp.broadcast_to(mine, (2 * PTS, N))
    loads[2].wait()
    row, col = iotas(2 * N, 2 * N)
    untie = as_bf16(col == 2 * (row % N) + row // N)
    for x in range(LOCAL):
        pair = dot(untie, lanes([coef[0, x], coef[1, x]]))
        for t in range(PTS):
            re = im = None
            for l in range(2):
                b_re, b_im = weight[l, pl.ds(t, 1)], weight[l, pl.ds(PTS + t, 1)]
                x_re = pair[:N, l * N : (l + 1) * N]
                x_im = pair[N:, l * N : (l + 1) * N]
                r, i = b_re * x_re - b_im * x_im, b_re * x_im + b_im * x_re
                re, im = (r, i) if re is None else (re + r, im + i)
            image_part[:, t, 0, x] = re.astype(BF16).reshape(RING, QUARTER, N)
            image_part[:, t, 1, x] = im.astype(BF16).reshape(RING, QUARTER, N)
    ring_start(image_part, image_land, image_sem)

    data_chunk(1)
    push_piece(2)

    def later_chunk(t, carry):
        data_chunk(t)
        return carry

    lax.fori_loop(2, PTS, later_chunk, 0)

    loads[3].wait()
    for x in range(LOCAL):
        both = dot(untie, lanes([maps[c, x] for c in range(LOCAL)]))
        sens_re[x] = both[:N]
        sens_im[x] = both[N:]
    ring_sum(image_part, image_land, image_half, image_sem, PTS)
    push_piece(3)
    loads[4].wait()
    for x in range(LOCAL):
        angle = (field[x] & (STEPS_CYCLE - 1)).astype(F32) * (2.0 * math.pi / STEPS_CYCLE)
        c1, s1 = jnp.cos(angle), jnp.sin(angle)
        c2, s2 = c1 * c1 - s1 * s1, 2.0 * (c1 * s1)
        c3, s3 = c2 * c1 - s2 * s1, s2 * c1 + c2 * s1
        c4, s4 = c2 * c2 - s2 * s2, 2.0 * (c2 * s2)
        for t, (c, s) in enumerate([(c1, s1), (c2, s2), (c3, s3), (c4, s4)]):
            cosine[t, x] = c
            sine[t, x] = s
    pair_sum(image_half, image_all, image_sem, PTS)
    arrive(0)
    push_piece(4)
    row, col = iotas(2 * N, 8 * N)
    spread = as_bf16(
        (row // N == col // (4 * N)) & (row % N == 4 * ((col % (4 * N)) // 16) + col % 4)
    )
    wide = dot(table[0], spread)
    for j in range(4):
        mix_y[j] = jnp.where((col // 4) % 4 == j, wide, 0.0).astype(BF16)

    mask_view = all_mask.at[pl.ds(0, SLABS - 1)]
    pltpu.make_async_copy(mask_view, mask_view, mask_recv).wait()
    all_mask[me] = own_mask[...]
    row, col = iotas(N, SLABS * 16)
    everything = all_mask[...].reshape(SLABS * 16, N)
    for t in range(PTS):
        pick = as_bf16((col // 16 == row // 4) & (col % 4 == row % 4) & ((col // 4) % 4 == t))
        mask_full[t] = dot(pick, everything)

    def model_term(t):
        def one(x, carry):
            i_re = image_all[:, t, 0, x].reshape(N, N).astype(F32)
            i_im = image_all[:, t, 1, x].reshape(N, N).astype(F32)
            c, s = cosine[t, x], sine[t, x]
            t_re, t_im = c * i_re - s * i_im, s * i_re + c * i_im
            s_re, s_im = sens_re[x], sens_im[x]
            stack = []
            for k in range(LOCAL):
                a, b = s_re[:, k * N : (k + 1) * N], s_im[:, k * N : (k + 1) * N]
                stack.append(lanes([(a * t_re - b * t_im).astype(BF16), (a * t_im + b * t_re).astype(BF16)]))
            depth = dot(rows_of(stack), table[0]).astype(BF16)
            planes = rows_of(
                [lanes([depth[k * N : (k + 1) * N, p * N : (p + 1) * N] for k in range(LOCAL)]) for p in range(2)]
            )
            lines = dot(table[1], planes)
            m = lanes([mask_full[t]] * LOCAL)
            lines = rows_of([(lines[:N] * m).astype(BF16), (lines[N:] * m).astype(BF16)])
            back = dot(table[0], lines).astype(BF16)
            stack = rows_of(
                [lanes([back[p * N : (p + 1) * N, k * N : (k + 1) * N] for p in range(2)]) for k in range(LOCAL)]
            )
            back = dot(stack, table[1])
            q_re = q_im = None
            for k in range(LOCAL):
                a, b = s_re[:, k * N : (k + 1) * N], s_im[:, k * N : (k + 1) * N]
                r, i = back[k * N : (k + 1) * N, :N], back[k * N : (k + 1) * N, N:]
                u, v = a * r + b * i, a * i - b * r
                q_re, q_im = (u, v) if q_re is None else (q_re + u, q_im + v)
            model[t, x, 0] = q_re
            model[t, x, 1] = q_im
            return carry

        lax.fori_loop(0, LOCAL, one, 0)

    def model_step(t, carry):
        model_term(t)
        return carry

    ring_end(image_all, image_sem)
    arrive(1)
    push_piece(5)
    lax.fori_loop(0, PTS, model_step, 0)

    def data_term(n):
        t, h = n // 2, n % 2

        def one(j, carry):
            x = 2 * h + j
            arrived = recv[t, :, h].reshape(SLABS * 16, 4 * N)
            q_re, q_im = model[t, x, 0], model[t, x, 1]
            for high in range(2):
                mix = mix_y[2 * high + j]
                plane = dot(mix[:, : 4 * N], arrived[:, : 2 * N]) + dot(mix[:, 4 * N :], arrived[:, 2 * N :])
                s_re = sens_re[x, :, pl.ds(high * 2 * N, 2 * N)]
                s_im = sens_im[x, :, pl.ds(high * 2 * N, 2 * N)]
                r, i = plane[:N], plane[N:]
                u, v = s_re * r + s_im * i, s_re * i - s_im * r
                q_re = q_re - u[:, :N] - u[:, N:]
                q_im = q_im - v[:, :N] - v[:, N:]
            comb_part[n, :, 0, j] = q_re.astype(BF16).reshape(RING, QUARTER, N)
            comb_part[n, :, 1, j] = q_im.astype(BF16).reshape(RING, QUARTER, N)
            return carry

        lax.fori_loop(0, 2, one, 0)
    def middle(n):
        ring_sum(comb_part.at[n], comb_land.at[n], comb_half.at[n], comb_sem.at[n], 2)

    def last(n):
        pair_sum(comb_half.at[n], comb_all.at[n], comb_sem.at[n], 2)

    def accumulate(n, final):
        t, h = n // 2, n % 2
        if not (final and n == PIECES - 1):
            ring_end(comb_all.at[n], comb_sem.at[n])
        for j in range(2):
            x = 2 * h + j
            q_re = comb_all[n, :, 0, j].reshape(N, N).astype(F32)
            q_im = comb_all[n, :, 1, j].reshape(N, N).astype(F32)
            c, s = cosine[t, x], sine[t, x]
            w_re, w_im = c * q_re + s * q_im, c * q_im - s * q_re
            for l in range(2):
                b_re, b_im = weight[l, pl.ds(t, 1)], weight[l, pl.ds(PTS + t, 1)]
                g_re = grad[l, x, 0] + (b_re * w_re + b_im * w_im)
                g_im = grad[l, x, 1] + (b_re * w_im - b_im * w_re)
                if final:
                    out_ref[l, x, pl.ds(0, N, stride=2), :] = g_re
                    out_ref[l, x, pl.ds(1, N, stride=2), :] = g_im
                else:
                    grad[l, x, 0] = g_re
                    grad[l, x, 1] = g_im

    grad[...] = jnp.zeros(grad.shape, F32)

    def begin(n):
        data_term(n)
        ring_start(comb_part.at[n], comb_land.at[n], comb_sem.at[n])

    arrive(2)
    push_piece(6)
    begin(0)
    begin(1)
    begin(2)
    arrive(3)
    begin(3)
    arrive(4)
    begin(4)
    for n in range(4):
        middle(n)
    arrive(5)
    begin(5)
    for n in range(4):
        last(n)
    middle(4)
    push_piece(7)
    arrive(6)
    begin(6)
    for n in range(4):
        accumulate(n, False)
    last(4)
    middle(5)
    arrive(7)
    data_term(PIECES - 1)
    end_part, end_all = comb_part.at[PIECES - 1], comb_all.at[PIECES - 1]

    def slot(ref, q, half):
        return ref.at[q, :, :, pl.ds(pl.multiple_of(half * ROWS, ROWS), ROWS)]

    def to_group(source, target, ssem, rsem):
        for across, k in ((1, 2), (1, 1), (1, 3), (0, 2), (1, 0), (0, 1), (0, 3)):
            to_side = lax.rem(side + across, 2)
            to = lax.rem(place + k, RING)
            pltpu.make_async_remote_copy(
                src_ref=source(to, to_side), dst_ref=target, send_sem=ssem, recv_sem=rsem,
                device_id=(me, to_side * RING + to), device_id_type=MESH,
            ).start()

    to_group(lambda q, half: slot(end_part, q, half), end_land.at[mg], end_sem.at[0], end_sem.at[1])
    middle(6)
    last(5)
    drain(end_land.at[pl.ds(0, GROUPS - 1)], end_sem.at[1])
    end_land[mg] = slot(end_part, place, side)[...]
    value = end_land[0].astype(F32)
    for j in range(1, GROUPS):
        value = value + end_land[j].astype(F32)
    slot(end_all, place, side)[...] = value.astype(BF16)
    mine = slot(end_all, place, side)
    to_group(lambda q, half: mine, mine, end_sem.at[2], end_sem.at[3])
    last(6)
    accumulate(4, False)
    accumulate(5, False)
    accumulate(6, True)
    drain(end_land.at[pl.ds(0, GROUPS - 1)], end_sem.at[3])
    accumulate(PIECES - 1, True)

    def spent(n, carry):
        drain(send.at[n // 2, pl.ds(0, SLABS - 1), lax.rem(n, 2)], send_sem.at[n])

        @pl.when(n < PIECES - 1)
        def _():
            ring_spent(comb_part.at[n], comb_half.at[n], comb_all.at[n], comb_sem.at[n])

        return carry

    lax.fori_loop(0, PIECES, spent, 0)
    ring_spent(image_part, image_half, image_all, image_sem)
    drain(end_land.at[pl.ds(0, GROUPS - 1)], end_sem.at[0])
    drain(end_land.at[pl.ds(0, GROUPS - 1)], end_sem.at[2])
    pltpu.make_async_copy(mask_view, mask_view, mask_send).wait()


def step(coef, basis, maps, field, data, mask):
    any_space = pl.BlockSpec(memory_space=pl.ANY)
    dma = pltpu.SemaphoreType.DMA
    image = (PTS, 2, LOCAL, QUARTER, N)
    comb = (2, 2, QUARTER, N)
    scratch = [
        pltpu.VMEM((2, LOCAL, 2 * N, N), BF16),
        pltpu.VMEM((2, PTS, 4 * PTS), BF16),
        pltpu.VMEM((LOCAL, LOCAL, 2 * N, N), BF16),
        pltpu.VMEM((LOCAL, N, N), I32),
        pltpu.VMEM((PTS, 4, N), I32),
        pltpu.VMEM((2, 2 * N, 2 * N), BF16),
        pltpu.VMEM((PTS, 8 * N, LOCAL * N), BF16),
        pltpu.VMEM((8 * N, 8 * N), BF16),
        pltpu.VMEM((4, 2 * N, 8 * N), BF16),
        pltpu.VMEM((PTS, SLABS, 2, 16, 4 * N), BF16),
        pltpu.VMEM((PTS, SLABS, 2, 16, 4 * N), BF16),
        pltpu.VMEM((16, N), BF16),
        pltpu.VMEM((SLABS, 16, N), BF16),
        pltpu.VMEM((PTS, N, N), F32),
        pltpu.VMEM((LOCAL, N, LOCAL * N), F32),
        pltpu.VMEM((LOCAL, N, LOCAL * N), F32),
        pltpu.VMEM((PTS, LOCAL, N, N), F32),
        pltpu.VMEM((PTS, LOCAL, N, N), F32),
        pltpu.VMEM((2, 2 * PTS, N), F32),
        pltpu.VMEM((PTS, LOCAL, 2, N, N), F32),
        pltpu.VMEM((2, LOCAL, 2, N, N), F32),
        pltpu.VMEM((RING,) + image, BF16),
        pltpu.VMEM((RING,) + image, BF16),
        pltpu.VMEM((2,) + image, BF16),
        pltpu.VMEM((RING,) + image, BF16),
        pltpu.VMEM((PIECES, RING) + comb, BF16),
        pltpu.VMEM((PIECES, RING) + comb, BF16),
        pltpu.VMEM((PIECES, 2) + comb, BF16),
        pltpu.VMEM((PIECES, RING) + comb, BF16),
        pltpu.VMEM((GROUPS, 2, 2, ROWS, N), BF16),
        dma((6,)), dma((PTS, LOCAL)), dma((PIECES,)), dma((PIECES,)), dma((PIECES,)), dma, dma,
        dma((6,)), dma((PIECES, 6)), dma((4,)),
    ]
    out = pl.pallas_call(
        body,
        out_shape=jax.ShapeDtypeStruct((2, LOCAL, 2 * N, N), F32),
        in_specs=[any_space] * 7,
        out_specs=pl.BlockSpec(memory_space=pltpu.VMEM),
        scratch_shapes=scratch,
        compiler_params=pltpu.CompilerParams(
            collective_id=0, has_side_effects=True, vmem_limit_bytes=44 << 20
        ),
    )(
        *[
            pltpu.with_memory_space_constraint(value, pltpu.HBM)
            for value in (
                coef.reshape(2, LOCAL, 2 * N, N),
                jnp.transpose(basis, (0, 2, 1)),
                maps.reshape(LOCAL, LOCAL, 2 * N, N),
                field,
                data.reshape(LOCAL, PTS, 8 * N, N),
                mask,
                jnp.asarray(dft_pair()),
            )
        ]
    )
    return out.reshape(2, LOCAL, N, 2, N)


def solution(mesh):
    in_specs = (
        P("coil", "space", None, None, None),
        P(),
        P("coil", "space", None, None, None),
        P("space", None, None),
        P("coil", None, None, "space", None, None),
        P(None, "space", None),
    )
    out_specs = P("coil", "space", None, None, None)
    return jax.shard_map(step, mesh=mesh, in_specs=in_specs, out_specs=out_specs, check_vma=False)
```
